128 devices in a mesh: tokens: 8 (over x_lo, y), tensor: 16 (over z, x_hi, core).
Axes of the slice: x: 4 (x_hi: 2, x_lo: 2; x = x_hi * 2 + x_lo), y: 4, z: 4, core: 2. Of those that a mesh axis runs over, the one named last changes fastest.
Arguments:
- codes: int32 [2, 6144, 5120], P(None, ('tokens', 'tensor')), may hold values from 0 to 254, as said below
- scales: int32 [2, 6144, 160], P(None, ('tokens', 'tensor')), may hold values from 119 to 122
- w_qkv: bfloat16 [5120, 15360], P(None, 'tensor'), may hold values from -0.078125 to 0.078125
- w_rate: bfloat16 [5120, 48], replicated, may hold values from -0.078125 to 0.078125
- rate_bias: float32 [48], P('tensor'), may hold values from -4 to 1
- fast_gate: float32 [16, 320, 320], P('tensor'), may hold values from -0.3125 to 0.3125
- fast_lift: float32 [16, 320, 320], P('tensor'), may hold values from -0.3125 to 0.3125
- fast_down: float32 [16, 320, 320], P('tensor'), may hold values from -0.3125 to 0.3125
- out_gain: float32 [5120], P('tensor'), may hold values from 0.5 to 1.5
Outputs:
- outputs: bfloat16 [2, 6144, 5120], P(None, 'tokens', 'tensor')
The draws below stay inside these ranges and needn't reach their ends.
Inputs may be any that keep to these rules, and one draw needn't show every extreme that they name: E4M3 codes: bit 7 is the sign, bits 3 to 6 the exponent, bits 0 to 2 the mantissa; 127 and 255 never occur.
All inputs are finite; a program needn't handle non-finite values.
Results may differ from the reference program's by a relative error of at most 0.039.
Values may be sent and summed in bfloat16 or wider, within the bound.
A program may use at most 128 MiB of HBM per device.

```python
import math
import jax
import jax.numpy as jnp
from jax import lax

H = 16
HD = 320
FH = 320
D = 5120
SPANS = 2
SPAN = 6144


def draw_codes(key, part):
    magnitude_key = jax.random.fold_in(key, 11)
    sign_key = jax.random.fold_in(key, 23)
    magnitude = jax.random.randint(magnitude_key, (SPANS, SPAN, D), 0, 127)
    negative = jax.random.randint(sign_key, (SPANS, SPAN, D), 0, 2)
    return (magnitude + 128 * negative).astype(jnp.int32)


def plant(entries, key, low, high):
    extent = entries.shape
    place = [jax.random.randint(jax.random.fold_in(key, axis), (), 0, extent[axis]) for axis in range(len(extent))]
    entries = entries.at[tuple(place)].set(low)
    longest = extent.index(max(extent))
    place[longest] = (place[longest] + 1) % extent[longest]
    return entries.at[tuple(place)].set(high)


def level_of(key, dims, shards, smallest, largest):
    def one(position, shards_of):
        draws = jax.random.uniform(jax.random.fold_in(jax.random.fold_in(key, 6), position), (shards_of,), jnp.float32, smallest / len(shards), largest / len(shards))
        return jnp.repeat(jnp.exp(draws), dims[position] // shards_of).reshape((-1,) + (1,) * (len(dims) - position - 1))

    level = one(*shards[0])
    for cut in shards[1:]:
        level = level * one(*cut)
    return level


def normal_values(stream_key, shape, deviation, most, split=(), kind=jnp.bfloat16):
    loudness = level_of(stream_key, shape, split, -0.22, 0.18) if split else 1.0
    result = jax.random.normal(stream_key, shape, jnp.float32) * deviation * loudness
    return jnp.minimum(jnp.maximum(result, -most), most).astype(kind)


def setup_inputs(seed: int = 0) -> dict:
    seeds = jax.random.split(jax.random.key(seed), 10)
    return {
        "codes": draw_codes(jax.random.fold_in(seeds[9], 71), 0),
        "scales": plant(jax.random.randint(seeds[1], (SPANS, SPAN, D // 32), 119, 123), jax.random.fold_in(seeds[1], 1), 119, 122).astype(jnp.int32),
        "w_qkv": normal_values(seeds[2], (D, 3 * D), D ** -0.5, 0.078125, ((1, 16),)),
        "w_rate": normal_values(seeds[3], (D, 3 * H), D ** -0.5, 0.078125),
        "rate_bias": jnp.clip(-4.0 + 5.0 * jax.random.uniform(seeds[4], (3 * H,), jnp.float32) ** level_of(seeds[4], (3 * H,), ((0, 16),), -0.2, 0.2), -4.0, 1.0),
        "fast_gate": normal_values(seeds[5], (H, HD, FH), HD ** -0.5, 0.3125, ((0, 16),), jnp.float32),
        "fast_lift": normal_values(seeds[6], (H, HD, FH), HD ** -0.5, 0.3125, ((0, 16),), jnp.float32),
        "fast_down": normal_values(seeds[7], (H, FH, HD), FH ** -0.5, 0.3125, ((0, 16),), jnp.float32),
        "out_gain": jnp.clip(1.0 + 0.1 * jax.random.normal(seeds[8], (D,), jnp.float32), 0.5, 1.5),
    }


epsilon = 1e-06
rate_base = 0.15

def dequantize(codes, scales):
    negative = jnp.where(codes >= 128, -1, 1).astype(jnp.int32)
    lower = codes % 128
    exponent = lower // 8
    mantissa = lower % 8
    significand = jnp.where(exponent == 0, mantissa, mantissa + 8) * negative
    shift_part = jnp.maximum(exponent, 1) - 1
    shape = codes.shape
    grouped = significand.reshape(shape[:-1] + (shape[-1] // 32, 32))
    shifts = shift_part.reshape(shape[:-1] + (shape[-1] // 32, 32)) + (scales - 119)[..., None]
    whole = grouped * jnp.left_shift(jnp.ones_like(shifts), shifts)
    values = whole.astype(jnp.float32) * (1.0 / 131072.0)
    return values.reshape(shape).astype(jnp.bfloat16)

def rms_norm(field):
    return field * lax.rsqrt(lax.optimization_barrier(jnp.mean(field * field, axis=-1, keepdims=True)) + epsilon)

def renorm(old, delta):
    summed = old + delta
    old_scale = jnp.sqrt(lax.optimization_barrier(jnp.mean(old * old, axis=-1, keepdims=True)) + epsilon)
    return summed * old_scale * lax.rsqrt(lax.optimization_barrier(jnp.mean(summed * summed, axis=-1, keepdims=True)) + epsilon)

def reference(codes, scales, w_qkv, w_rate, rate_bias, fast_gate, fast_lift, fast_down, out_gain):
    activations = dequantize(codes, scales)
    rate_logits = jnp.dot(activations, w_rate, preferred_element_type=jnp.float32)
    factor = rate_base / math.sqrt(SPAN)

    def head_pass(head_idx):
        columns = lax.dynamic_slice_in_dim(w_qkv, head_idx * (3 * HD), 3 * HD, 1)
        logits = lax.dynamic_slice_in_dim(rate_logits, head_idx * 3, 3, 2)
        bias = lax.dynamic_slice_in_dim(rate_bias, head_idx * 3, 3, 0)
        gain = lax.dynamic_slice_in_dim(out_gain, head_idx * HD, HD, 0)
        gate_w = fast_gate[head_idx]
        lift_w = fast_lift[head_idx]
        down_w = fast_down[head_idx]
        results = []
        for block in range(SPANS):
            projected = jnp.dot(activations[block], columns, preferred_element_type=jnp.float32).astype(jnp.bfloat16)
            queries = projected[:, :HD]
            key_rows = projected[:, HD:2 * HD]
            value_rows = projected[:, 2 * HD:]
            query_norm = rms_norm(queries.astype(jnp.float32)).astype(jnp.bfloat16)
            key_norm = rms_norm(key_rows.astype(jnp.float32)).astype(jnp.bfloat16)
            rates_now = jax.nn.softplus(logits[block] + bias) * factor
            gate_b = gate_w.astype(jnp.bfloat16)
            lift_b = lift_w.astype(jnp.bfloat16)
            down_b = down_w.astype(jnp.bfloat16)
            gate_pre = jnp.dot(key_norm, gate_b, preferred_element_type=jnp.float32)
            lift_pre = jnp.dot(key_norm, lift_b, preferred_element_type=jnp.float32)
            gate_sig = jax.nn.sigmoid(gate_pre)
            activated = gate_pre * gate_sig
            hidden = (activated * lift_pre).astype(jnp.bfloat16)
            hidden_grad = jnp.dot(value_rows, down_b.T, preferred_element_type=jnp.float32)
            gate_grad = (hidden_grad * lift_pre * gate_sig * (1.0 + gate_pre * (1.0 - gate_sig))).astype(jnp.bfloat16)
            lift_grad = (hidden_grad * activated).astype(jnp.bfloat16)
            key_gate = (key_norm.astype(jnp.float32) * rates_now[:, 0:1]).astype(jnp.bfloat16)
            key_lift = (key_norm.astype(jnp.float32) * rates_now[:, 1:2]).astype(jnp.bfloat16)
            hidden_rate = (hidden.astype(jnp.float32) * rates_now[:, 2:3]).astype(jnp.bfloat16)
            delta_gate = jnp.dot(key_gate.T, gate_grad, preferred_element_type=jnp.float32)
            delta_lift = jnp.dot(key_lift.T, lift_grad, preferred_element_type=jnp.float32)
            delta_down = jnp.dot(hidden_rate.T, value_rows, preferred_element_type=jnp.float32)
            gate_w = renorm(gate_w, delta_gate)
            lift_w = renorm(lift_w, delta_lift)
            down_w = renorm(down_w, delta_down)
            query_gate = jnp.dot(query_norm, gate_w.astype(jnp.bfloat16), preferred_element_type=jnp.float32)
            query_lift = jnp.dot(query_norm, lift_w.astype(jnp.bfloat16), preferred_element_type=jnp.float32)
            query_hidden = (jax.nn.silu(query_gate) * query_lift).astype(jnp.bfloat16)
            fast_out = jnp.dot(query_hidden, down_w.astype(jnp.bfloat16), preferred_element_type=jnp.float32)
            results.append((rms_norm(fast_out) * gain).astype(jnp.bfloat16))
        return jnp.stack(results, 0)
    per_head = lax.map(head_pass, jnp.arange(H, dtype=jnp.int32))
    return jnp.transpose(per_head, (1, 2, 0, 3)).reshape(SPANS, SPAN, D)
```

```python
import functools
import math

import jax
import jax.numpy as jnp
from jax import lax
from jax.experimental import pallas as pl
from jax.experimental.pallas import tpu as pltpu
from jax.sharding import PartitionSpec as P

epsilon = 1e-06
rate_base = 0.15

MESH = pl.DeviceIdType.MESH
BF = jnp.bfloat16
F32 = jnp.float32

UNIT = 16
HALVES = 2
AHEAD = 1
LAG = 2
KEYS = 384
PAD = 64


def dot(a, b):
    return jnp.dot(a, b, preferred_element_type=F32)


def dot_tn(a, b):
    return lax.dot_general(a, b, (((0,), (0,)), ((), ())), preferred_element_type=F32)


def dot_nt(a, b):
    return lax.dot_general(a, b, (((1,), (1,)), ((), ())), preferred_element_type=F32)


def kernel(
    factor,
    codes_hbm,
    scales_ref,
    wqkv_hbm,
    wrate_hbm,
    bias_ref,
    gate_ref,
    lift_ref,
    down_ref,
    gain_ref,
    out_ref,
    acts,
    w,
    w_rate,
    w_last,
    codes,
    spread,
    factors,
    acc,
    stack,
    master,
    rs_send,
    rs_recv,
    fast,
    queries,
    keys,
    values,
    rates,
    local_sem,
    send_sem,
    z_sem,
    x_sem,
    part_a_sem,
    part_b_sem,
    near_sem,
    far_sem,
    rs_send_sem,
    rs_sem,
    ag_send_sem,
    ag_sem,
):
    rounds, sources, unit, width = acts.shape
    units = rounds // HALVES
    part_a = width * 2 // 5 // 128 * 128
    depth = w.shape[0]
    head = gate_ref.shape[1]
    tokens = sources * unit
    t = lax.axis_index("tokens")
    h = lax.axis_index("tensor")
    shards = 8
    z, hi, core = h // 4, (h // 2) % 2, h % 2

    def at(dz, other):
        side = 1 - hi if other else hi
        return lax.rem(z + dz, 4) * 4 + side * 2 + core

    z_peers = [at(dz, False) for dz in (1, 3, 2)]
    x_peer = at(0, True)
    diagonal = [at(dz, True) for dz in (1, 3, 2)]
    sibling = h + 1 - 2 * core
    t_peers = [lax.rem(t + k, shards) for k in range(1, shards)]

    barrier = pltpu.get_barrier_semaphore()
    for peer in z_peers + [x_peer, sibling]:
        pl.semaphore_signal(barrier, inc=1, device_id=(t, peer), device_id_type=MESH)
    for peer in t_peers:
        pl.semaphore_signal(barrier, inc=1, device_id=(peer, h), device_id_type=MESH)

    codes_copy = pltpu.make_async_copy(codes_hbm, codes, local_sem.at[0])
    w_copy = pltpu.make_async_copy(wqkv_hbm, w, local_sem.at[1])
    rate_copy = pltpu.make_async_copy(wrate_hbm, w_rate, local_sem.at[2])
    codes_copy.start()
    w_copy.start()
    rate_copy.start()

    groups = scales_ref.shape[1]
    group = lax.broadcasted_iota(jnp.int32, (groups, depth), 0)
    column = lax.broadcasted_iota(jnp.int32, (groups, depth), 1)
    spread[...] = jnp.where(
        lax.shift_right_logical(column, 5) == group, 1.0, 0.0
    ).astype(BF)
    powers = lax.shift_left(jnp.ones_like(scales_ref[...]), scales_ref[...] - 119)
    powers = powers.astype(F32).astype(BF)
    step_n = 512

    def spread_step(n, carry):
        cols = pl.ds(pl.multiple_of(n * step_n, step_n), step_n)
        factors[:, cols] = dot(powers, spread[:, cols]) * (1.0 / 131072.0)
        return carry

    lax.fori_loop(0, depth // step_n, spread_step, 0)
    codes_copy.wait()

    def decode(r, carry):
        rows = pl.ds(pl.multiple_of((r // HALVES) * unit, unit), unit)
        for n in range(width // step_n):
            start = (r % HALVES) * width + n * step_n
            cols = pl.ds(pl.multiple_of(start, step_n), step_n)
            code = codes[rows, cols]
            lower = jnp.bitwise_and(code, 127)
            exponent = lax.shift_right_logical(lower, 3)
            mantissa = jnp.bitwise_and(lower, 7)
            normal = exponent > 0
            significand = jnp.where(normal, mantissa + 8, mantissa)
            significand = jnp.where(code >= 128, -significand, significand)
            shift = jnp.where(normal, exponent - 1, 0)
            whole = lax.shift_left(significand, shift).astype(F32)
            acts[r, h, :, n * step_n : (n + 1) * step_n] = (
                whole * factors[rows, cols]
            ).astype(BF)
        return carry

    def remote(src, dst, send, recv, tok, ten):
        pltpu.make_async_remote_copy(
            src_ref=src,
            dst_ref=dst,
            send_sem=send,
            recv_sem=recv,
            device_id=(tok, ten),
            device_id_type=MESH,
        ).start()

    def wait(ref, sem):
        pltpu.make_async_copy(ref, ref, sem).wait()

    def send_own(s):
        mine = acts.at[s, h]
        for peer in z_peers:
            remote(mine, mine, send_sem.at[s], z_sem.at[s], t, peer)
        remote(mine, mine, send_sem.at[s], x_sem.at[s], t, x_peer)
        remote(mine, mine, send_sem.at[s], near_sem.at[s], t, sibling)

    def forward(s):
        wait(acts.at[s, 0:3], z_sem.at[s])
        for peer in z_peers:
            part = acts.at[s, peer, :, part_a:width]
            remote(part, part, send_sem.at[s], part_b_sem.at[s], t, x_peer)
        for peer in z_peers:
            item = acts.at[s, peer]
            remote(item, item, send_sem.at[s], near_sem.at[s], t, sibling)
        wait(acts.at[s, 0], x_sem.at[s])
        part = acts.at[s, x_peer, :, 0:part_a]
        for peer in z_peers:
            remote(part, part, send_sem.at[s], part_a_sem.at[s], t, peer)
        item = acts.at[s, x_peer]
        remote(item, item, send_sem.at[s], near_sem.at[s], t, sibling)

    def forward_far(s):
        wait(acts.at[s, 0:3, :, 0:part_a], part_a_sem.at[s])
        wait(acts.at[s, 0:3, :, part_a:width], part_b_sem.at[s])
        for peer in diagonal:
            item = acts.at[s, peer]
            remote(item, item, send_sem.at[s], far_sem.at[s], t, sibling)

    decode(0, 0)
    pl.semaphore_wait(barrier, 12)
    for s in range(AHEAD):
        if s > 0:
            decode(s, 0)
        send_own(s)
    lax.fori_loop(AHEAD, rounds, decode, 0)

    stack[...] = jnp.zeros_like(stack)
    stack[PAD : PAD + head, 0:head] = gate_ref[0]
    stack[PAD + head : PAD + 2 * head, 0:head] = lift_ref[0]
    stack[PAD + 2 * head : PAD + 3 * head, 0:head] = down_ref[0]
    fast[0] = stack[...].astype(BF)
    shard = stack.shape[0] // shards
    own_rows = pl.ds(pl.multiple_of(t * shard, shard), shard)
    master[...] = stack[own_rows, :]
    stack[...] = jnp.zeros_like(stack)

    w_copy.wait()
    rate_copy.wait()
    main = 3 * head // 256 * 256
    tail = 3 * head - main
    rate_cols = w_rate.shape[1]

    def last_step(n, carry):
        rows = pl.ds(pl.multiple_of(n * 512, 512), 512)
        w_last[rows, :] = jnp.concatenate(
            [
                w[rows, main : 3 * head],
                w_rate[rows, :],
                jnp.zeros((512, 256 - tail - rate_cols), BF),
            ],
            axis=1,
        )
        return carry

    lax.fori_loop(0, depth // 512, last_step, 0)

    def project(c, half):
        chunk = 512

        def one(k, carry):
            cols = pl.ds(pl.multiple_of(k * chunk, chunk), chunk)
            rows = pl.ds(pl.multiple_of(half * width + k * chunk, chunk), chunk)
            x = acts[c, :, :, cols].reshape(tokens, chunk)
            acc[:, 0:main] += dot(x, w[rows, 0:main])
            acc[:, main : main + 256] += dot(x, w_last[rows, :])
            return carry

        @pl.when(half == 0)
        def _():
            acc[...] = jnp.zeros_like(acc)

        lax.fori_loop(0, width // chunk, one, 0)

    def finish(u):
        q = acc[:, 0:head]
        q = q * lax.rsqrt(jnp.sum(q * q, axis=1, keepdims=True) * (1.0 / head) + epsilon)
        queries[u] = q.astype(BF)
        k = acc[:, head - PAD : 2 * head]
        lane = lax.broadcasted_iota(jnp.int32, k.shape, 1)
        k = jnp.where(lane >= PAD, k, 0.0)
        k = k * lax.rsqrt(jnp.sum(k * k, axis=1, keepdims=True) * (1.0 / head) + epsilon)
        keys[u] = k.astype(BF)
        values[u] = acc[:, 2 * head : 3 * head].astype(BF)
        logits = acc[:, main + 128 : main + 256]
        lane = lax.broadcasted_iota(jnp.int32, logits.shape, 1)
        first = tail - 128 + 3 * h
        picked = jnp.zeros(logits.shape, F32)
        for i in range(3):
            mine = jnp.where(lane == first + i, logits, 0.0)
            column = jnp.sum(mine, axis=1, keepdims=True) + bias_ref[0, i]
            picked = jnp.where(lane == i, column, picked)
        soft = jnp.maximum(picked, 0.0) + jnp.log1p(jnp.exp(-jnp.abs(picked)))
        rates[u] = soft * factor

    def key_step(u, carry):
        version = u // (units // 2)
        kn = keys[u]
        v = values[u]
        rate = rates[u]
        gate_pre = dot(kn, fast[version, 0:KEYS, 0:head])
        lift_pre = dot(kn, fast[version, head : head + KEYS, 0:head])
        hidden_grad = dot_nt(v, fast[version, PAD + 2 * head : PAD + 3 * head, 0:head])
        sig = jax.nn.sigmoid(gate_pre)
        activated = gate_pre * sig
        hidden = activated * lift_pre
        gate_grad = hidden_grad * lift_pre * (sig * (1.0 + gate_pre * (1.0 - sig)))
        lift_grad = hidden_grad * activated
        gate_grad = (gate_grad * rate[:, 0:1]).astype(BF)
        lift_grad = (lift_grad * rate[:, 1:2]).astype(BF)
        hidden = (hidden * rate[:, 2:3]).astype(BF)
        stack[0:KEYS, 0:head] += dot_tn(kn, gate_grad)
        stack[KEYS : KEYS + head, 0:head] += dot_tn(kn, lift_grad)[PAD:KEYS]
        stack[KEYS + head : KEYS + 2 * head, 0:head] += dot_tn(hidden, v)
        return carry

    def reduce_send(block):
        rs_send[...] = stack[...].astype(BF)
        stack[...] = jnp.zeros_like(stack)
        for peer in t_peers:
            rows = pl.ds(pl.multiple_of(peer * shard, shard), shard)
            remote(
                rs_send.at[rows],
                rs_recv.at[block, t],
                rs_send_sem.at[block],
                rs_sem.at[block],
                peer,
                h,
            )
        rs_recv[block, t] = rs_send[own_rows, :]

    def reduce_finish(block):
        wait(rs_recv.at[block, 0:7], rs_sem.at[block])
        wait(rs_send.at[0 : 7 * shard], rs_send_sem.at[block])
        summed = rs_recv[block, 0].astype(F32)
        for j in range(1, shards):
            summed = summed + rs_recv[block, j].astype(F32)
        old = master[...]
        summed = old + summed
        old_scale = jnp.sqrt(
            jnp.sum(old * old, axis=1, keepdims=True) * (1.0 / head) + epsilon
        )
        new_scale = lax.rsqrt(
            jnp.sum(summed * summed, axis=1, keepdims=True) * (1.0 / head) + epsilon
        )
        new = summed * old_scale * new_scale
        master[...] = new
        fast[block + 1, own_rows, :] = new.astype(BF)
        mine = fast.at[block + 1, own_rows]
        for peer in t_peers:
            remote(mine, mine, ag_send_sem.at[block], ag_sem.at[block], peer, h)

    def gather_finish(block):
        wait(fast.at[block + 1, 0 : 7 * shard], ag_sem.at[block])
        wait(fast.at[block + 1, 0 : 7 * shard], ag_send_sem.at[block])

    def query_step(u, carry):
        block = u // (units // 2)
        q = queries[u]
        gate_pre = dot(q, fast[block + 1, PAD : PAD + head, 0:head])
        lift_pre = dot(q, fast[block + 1, PAD + head : PAD + 2 * head, 0:head])
        hidden = (gate_pre * jax.nn.sigmoid(gate_pre) * lift_pre).astype(BF)
        out = dot(hidden, fast[block + 1, PAD + 2 * head : PAD + 3 * head, 0:head])
        out = out * lax.rsqrt(
            jnp.sum(out * out, axis=1, keepdims=True) * (1.0 / head) + epsilon
        )
        out = (out * gain_ref[...]).astype(BF)
        out_ref[block, :, u % (units // 2)] = out.reshape(sources, unit, head)
        return carry

    per_block = rounds // 2

    def step(s, carry):
        @pl.when(s + AHEAD < rounds)
        def _():
            send_own(s + AHEAD)

        @pl.when(s < rounds)
        def _():
            forward(s)

        @pl.when((s >= 1) & (s < rounds + 1))
        def _():
            forward_far(s - 1)

        c = s - LAG

        @pl.when(c >= 0)
        def _():
            wait(acts.at[c, 0:5], near_sem.at[c])
            wait(acts.at[c, 0:3], far_sem.at[c])
            half = c % HALVES
            u = c // HALVES
            project(c, half)

            @pl.when(half == HALVES - 1)
            def _():
                finish(u)

            @pl.when(c == per_block + 1)
            def _():
                reduce_finish(0)

            @pl.when(c == per_block + 3)
            def _():
                gather_finish(0)

            first = jnp.where(c == per_block + 3, units // 2, u)
            ready = (half == HALVES - 1) & (c != per_block + 1)
            lax.fori_loop(first, jnp.where(ready, u + 1, first), key_step, 0)

            @pl.when(c == per_block - 1)
            def _():
                reduce_send(0)

        return carry

    lax.fori_loop(0, rounds + LAG, step, 0)
    reduce_send(1)
    lax.fori_loop(0, units // 2, query_step, 0)

    def drain(s, carry):
        wait(acts.at[s, 0:15], send_sem.at[s])
        return carry

    lax.fori_loop(0, rounds, drain, 0)
    reduce_finish(1)
    gather_finish(1)
    lax.fori_loop(units // 2, units, query_step, 0)


def local(codes, scales, w_qkv, w_rate, rate_bias, fast_gate, fast_lift, fast_down, out_gain):
    blocks, rows, depth = codes.shape
    head = fast_gate.shape[1]
    sources = lax.axis_size("tensor")
    shards = lax.axis_size("tokens")
    units = blocks * rows // UNIT
    rounds = units * HALVES
    tokens = sources * UNIT
    width = depth // HALVES
    factor = rate_base / math.sqrt(rows * sources * shards)
    stacked = 3 * head + PAD
    vmem = pl.BlockSpec(memory_space=pltpu.VMEM)
    smem = pl.BlockSpec(memory_space=pltpu.SMEM)
    anyspace = pl.BlockSpec(memory_space=pl.ANY)
    dma = pltpu.SemaphoreType.DMA
    out = pl.pallas_call(
        functools.partial(kernel, factor),
        out_shape=jax.ShapeDtypeStruct((blocks, sources, rows // UNIT, UNIT, head), BF),
        in_specs=[anyspace, vmem, anyspace, anyspace, smem, vmem, vmem, vmem, vmem],
        out_specs=vmem,
        scratch_shapes=[
            pltpu.VMEM((rounds, sources, UNIT, width), BF),
            pltpu.VMEM((depth, 3 * head), BF),
            pltpu.VMEM((depth, w_rate.shape[1]), BF),
            pltpu.VMEM((depth, 256), BF),
            pltpu.VMEM((blocks * rows, depth), jnp.int32),
            pltpu.VMEM((scales.shape[2], depth), BF),
            pltpu.VMEM((blocks * rows, depth), F32),
            pltpu.VMEM((tokens, 1024), F32),
            pltpu.VMEM((stacked, KEYS), F32),
            pltpu.VMEM((stacked // shards, KEYS), F32),
            pltpu.VMEM((stacked, KEYS), BF),
            pltpu.VMEM((2, shards, stacked // shards, KEYS), BF),
            pltpu.VMEM((3, stacked, KEYS), BF),
            pltpu.VMEM((units, tokens, head), BF),
            pltpu.VMEM((units, tokens, KEYS), BF),
            pltpu.VMEM((units, tokens, head), BF),
            pltpu.VMEM((units, tokens, 128), F32),
            dma((3,)),
            dma((rounds,)),
            dma((rounds,)),
            dma((rounds,)),
            dma((rounds,)),
            dma((rounds,)),
            dma((rounds,)),
            dma((rounds,)),
            dma((2,)),
            dma((2,)),
            dma((2,)),
            dma((2,)),
        ],
        compiler_params=pltpu.CompilerParams(
            collective_id=0, has_side_effects=True, vmem_limit_bytes=58 << 20
        ),
        name="fast_weights",
    )(
        codes.reshape(blocks * rows, depth),
        scales.reshape(blocks * rows, scales.shape[2]),
        w_qkv,
        w_rate,
        rate_bias.reshape(1, 3),
        fast_gate,
        fast_lift,
        fast_down,
        out_gain.reshape(1, head),
    )
    return out.reshape(blocks, sources * rows, head)


def solution(mesh):
    return jax.shard_map(
        local,
        mesh=mesh,
        in_specs=(
            P(None, ("tokens", "tensor"), None),
            P(None, ("tokens", "tensor"), None),
            P(None, "tensor"),
            P(),
            P("tensor"),
            P("tensor", None, None),
            P("tensor", None, None),
            P("tensor", None, None),
            P("tensor"),
        ),
        out_specs=P(None, "tokens", "tensor"),
        check_vma=False,
    )
```

```python
import functools
import math

import jax
import jax.numpy as jnp
from jax import lax
from jax.experimental import pallas as pl
from jax.experimental.pallas import tpu as pltpu
from jax.sharding import PartitionSpec as P

epsilon = 1e-06
rate_base = 0.15

MESH = pl.DeviceIdType.MESH
BF = jnp.bfloat16
F32 = jnp.float32

UNIT = 16
HALVES = 2
AHEAD = 1
LAG = 2
KEYS = 384
PAD = 64


def dot(a, b):
    return jnp.dot(a, b, preferred_element_type=F32)


def dot_nt(a, b):
    return lax.dot_general(a, b, (((1,), (1,)), ((), ())), preferred_element_type=F32)


def flip(a):
    return a.astype(F32).T.astype(BF)


def kernel(
    factor,
    codes_hbm,
    scales_ref,
    wqkv_hbm,
    wrate_hbm,
    bias_ref,
    gate_ref,
    lift_ref,
    down_ref,
    gain_ref,
    out_ref,
    acts,
    w,
    codes,
    spread,
    factors,
    kv_acc,
    q_acc,
    stack,
    master,
    rs_send,
    rs_recv,
    fast,
    gate_lift,
    gains,
    queries,
    keys,
    values,
    rates,
    local_sem,
    send_sem,
    z_sem,
    x_sem,
    part_a_sem,
    part_b_sem,
    near_sem,
    far_sem,
    rs_send_sem,
    rs_sem,
    ag_send_sem,
    ag_sem,
):
    blocks, _, sources, rows_dev, width = acts.shape
    per = rows_dev // UNIT
    units = blocks * per
    rounds = units * HALVES
    part_a = width * 2 // 5 // 128 * 128
    depth = w.shape[1]
    head = gate_ref.shape[1]
    tokens = sources * UNIT
    block_tokens = sources * rows_dev
    chunk = 1280
    t = lax.axis_index("tokens")
    h = lax.axis_index("tensor")
    shards = 8
    z, hi, core = h // 4, (h // 2) % 2, h % 2

    def at(dz, other):
        side = 1 - hi if other else hi
        return lax.rem(z + dz, 4) * 4 + side * 2 + core

    z_peers = [at(dz, False) for dz in (1, 3, 2)]
    x_peer = at(0, True)
    diagonal = [at(dz, True) for dz in (1, 3, 2)]
    sibling = h + 1 - 2 * core
    t_peers = [lax.rem(t + k, shards) for k in range(1, shards)]

    barrier = pltpu.get_barrier_semaphore()
    for peer in z_peers + [x_peer, sibling]:
        pl.semaphore_signal(barrier, inc=1, device_id=(t, peer), device_id_type=MESH)
    for peer in t_peers:
        pl.semaphore_signal(barrier, inc=1, device_id=(peer, h), device_id_type=MESH)

    codes_copy = pltpu.make_async_copy(codes_hbm, codes, local_sem.at[0])
    w_copy = pltpu.make_async_copy(wqkv_hbm, w.at[0 : 3 * head], local_sem.at[1])
    rate_copy = pltpu.make_async_copy(
        wrate_hbm, w.at[3 * head : w.shape[0]], local_sem.at[2]
    )
    codes_copy.start()
    w_copy.start()
    rate_copy.start()

    groups = scales_ref.shape[1]
    group = lax.broadcasted_iota(jnp.int32, (groups, depth), 0)
    column = lax.broadcasted_iota(jnp.int32, (groups, depth), 1)
    spread[...] = jnp.where(
        lax.shift_right_logical(column, 5) == group, 1.0, 0.0
    ).astype(BF)
    powers = lax.shift_left(jnp.ones_like(scales_ref[...]), scales_ref[...] - 119)
    powers = powers.astype(F32).astype(BF)
    step_n = 512

    def spread_step(n, carry):
        cols = pl.ds(pl.multiple_of(n * step_n, step_n), step_n)
        factors[:, cols] = dot(powers, spread[:, cols]) * (1.0 / 131072.0)
        return carry

    lax.fori_loop(0, depth // step_n, spread_step, 0)
    codes_copy.wait()

    def place(s):
        u = s // HALVES
        return u // per, s % HALVES, pl.ds(pl.multiple_of((u % per) * UNIT, UNIT), UNIT)

    def item(s, source):
        block, half, rows = place(s)
        return acts.at[block, half, source, rows]

    def decode(s, carry):
        block, half, unit_rows = place(s)
        rows = pl.ds(pl.multiple_of((s // HALVES) * UNIT, UNIT), UNIT)
        for n in range(width // step_n):
            start = half * width + n * step_n
            cols = pl.ds(pl.multiple_of(start, step_n), step_n)
            code = codes[rows, cols]
            lower = jnp.bitwise_and(code, 127)
            exponent = lax.shift_right_logical(lower, 3)
            mantissa = jnp.bitwise_and(lower, 7)
            normal = exponent > 0
            significand = jnp.where(normal, mantissa + 8, mantissa)
            significand = jnp.where(code >= 128, -significand, significand)
            shift = jnp.where(normal, exponent - 1, 0)
            whole = lax.shift_left(significand, shift).astype(F32)
            acts[block, half, h, unit_rows, n * step_n : (n + 1) * step_n] = (
                whole * factors[rows, cols]
            ).astype(BF)
        return carry

    def remote(src, dst, send, recv, tok, ten):
        pltpu.make_async_remote_copy(
            src_ref=src,
            dst_ref=dst,
            send_sem=send,
            recv_sem=recv,
            device_id=(tok, ten),
            device_id_type=MESH,
        ).start()

    def wait(ref, sem):
        pltpu.make_async_copy(ref, ref, sem).wait()

    def several(n, first=0, last=width):
        return acts.at[0, 0, 0:n, 0:UNIT, first:last]

    def send_own(s):
        mine = item(s, h)
        for peer in z_peers:
            remote(mine, mine, send_sem.at[s], z_sem.at[s], t, peer)
        remote(mine, mine, send_sem.at[s], x_sem.at[s], t, x_peer)
        remote(mine, mine, send_sem.at[s], near_sem.at[s], t, sibling)

    def forward(s):
        wait(several(3), z_sem.at[s])
        for peer in z_peers:
            part = item(s, peer).at[:, part_a:width]
            remote(part, part, send_sem.at[s], part_b_sem.at[s], t, x_peer)
        for peer in z_peers:
            whole = item(s, peer)
            remote(whole, whole, send_sem.at[s], near_sem.at[s], t, sibling)
        wait(several(1), x_sem.at[s])
        part = item(s, x_peer).at[:, 0:part_a]
        for peer in z_peers:
            remote(part, part, send_sem.at[s], part_a_sem.at[s], t, peer)
        whole = item(s, x_peer)
        remote(whole, whole, send_sem.at[s], near_sem.at[s], t, sibling)

    def forward_far(s):
        wait(several(3, 0, part_a), part_a_sem.at[s])
        wait(several(3, part_a, width), part_b_sem.at[s])
        for peer in diagonal:
            whole = item(s, peer)
            remote(whole, whole, send_sem.at[s], far_sem.at[s], t, sibling)

    decode(0, 0)
    pl.semaphore_wait(barrier, 12)
    for s in range(AHEAD):
        if s > 0:
            decode(s, 0)
        send_own(s)
    lax.fori_loop(AHEAD, rounds, decode, 0)

    stack[...] = jnp.zeros_like(stack)
    stack[0:head, 0:head] = gate_ref[0]
    stack[head : 2 * head, 0:head] = lift_ref[0]
    stack[2 * head : 3 * head, 0:head] = down_ref[0]
    fast[0] = stack[...].astype(BF)
    shard = stack.shape[0] // shards
    own_rows = pl.ds(pl.multiple_of(t * shard, shard), shard)
    master[...] = stack[own_rows, :]
    stack[...] = jnp.zeros_like(stack)
    gains[...] = jnp.broadcast_to(gain_ref[...][None, :], (128, head)).T

    def turn(version):
        gate_lift[version, 0:head] = flip(fast[version, 0:head, 0:head])
        gate_lift[version, head : 2 * head] = flip(fast[version, head : 2 * head, 0:head])

    turn(0)
    w_copy.wait()
    rate_copy.wait()

    def project_keys(c):
        block, half, rows = place(c)

        def one(k, carry):
            cols = pl.ds(pl.multiple_of(k * chunk, chunk), chunk)
            deep = pl.ds(pl.multiple_of(half * width + k * chunk, chunk), chunk)
            x = acts[block, half, :, rows, cols].reshape(tokens, chunk)
            kv_acc[...] += dot_nt(w[head : w.shape[0], deep], x)
            return carry

        @pl.when(half == 0)
        def _():
            kv_acc[...] = jnp.zeros_like(kv_acc)

        lax.fori_loop(0, width // chunk, one, 0)

    def project_queries(block):
        def one(k, carry):
            half = k // (width // chunk)
            start = (k % (width // chunk)) * chunk
            cols = pl.ds(pl.multiple_of(start, chunk), chunk)
            deep = pl.ds(pl.multiple_of(k * chunk, chunk), chunk)
            x = acts[block, half, :, :, cols].reshape(block_tokens, chunk)
            q_acc[...] += dot_nt(w[0:head, deep], x)
            return carry

        q_acc[...] = jnp.zeros_like(q_acc)
        lax.fori_loop(0, depth // chunk, one, 0)
        for n in range(block_tokens // 256):
            q = q_acc[:, n * 256 : (n + 1) * 256]
            q = q * lax.rsqrt(
                jnp.sum(q * q, axis=0, keepdims=True) * (1.0 / head) + epsilon
            )
            queries[block, n * 256 : (n + 1) * 256] = q.T.astype(BF)

    def finish_keys(u):
        k = kv_acc[0:head]
        k = k * lax.rsqrt(jnp.sum(k * k, axis=0, keepdims=True) * (1.0 / head) + epsilon)
        keys[u] = k.astype(BF)
        values[u] = kv_acc[head : 2 * head].astype(BF)
        for i in range(3):
            logit = kv_acc[pl.ds(2 * head + 3 * h + i, 1), :] + bias_ref[0, i]
            soft = jnp.maximum(logit, 0.0) + jnp.log1p(jnp.exp(-jnp.abs(logit)))
            rates[u, i : i + 1] = soft * factor

    def key_step(u, carry):
        version = u // per
        kn = keys[u]
        v = values[u]
        pre = dot(gate_lift[version], kn)
        gate_pre = pre[0:head]
        lift_pre = pre[head : 2 * head]
        hidden_grad = dot(fast[version, 2 * head : 3 * head, 0:head], v)
        sig = jax.nn.sigmoid(gate_pre)
        activated = gate_pre * sig
        hidden = activated * lift_pre
        gate_grad = hidden_grad * lift_pre * (sig * (1.0 + gate_pre * (1.0 - sig)))
        lift_grad = hidden_grad * activated
        gate_grad = (gate_grad * rates[u, 0:1]).astype(BF)
        lift_grad = (lift_grad * rates[u, 1:2]).astype(BF)
        hidden = (hidden * rates[u, 2:3]).astype(BF)
        stack[0:head, 0:head] += dot_nt(kn, gate_grad)
        stack[head : 2 * head, 0:head] += dot_nt(kn, lift_grad)
        stack[2 * head : 3 * head, 0:head] += dot_nt(hidden, v)
        return carry

    def reduce_send(block):
        rs_send[...] = stack[...].astype(BF)
        for peer in t_peers:
            rows = pl.ds(pl.multiple_of(peer * shard, shard), shard)
            remote(
                rs_send.at[rows],
                rs_recv.at[block, t],
                rs_send_sem.at[block],
                rs_sem.at[block],
                peer,
                h,
            )
        rs_recv[block, t] = rs_send[own_rows, :]
        stack[...] = jnp.zeros_like(stack)

    def reduce_finish(block):
        wait(rs_recv.at[block, 0:7], rs_sem.at[block])
        wait(rs_send.at[0 : 7 * shard], rs_send_sem.at[block])
        summed = rs_recv[block, 0].astype(F32)
        for j in range(1, shards):
            summed = summed + rs_recv[block, j].astype(F32)
        old = master[...]
        summed = old + summed
        old_scale = jnp.sqrt(
            jnp.sum(old * old, axis=1, keepdims=True) * (1.0 / head) + epsilon
        )
        new_scale = lax.rsqrt(
            jnp.sum(summed * summed, axis=1, keepdims=True) * (1.0 / head) + epsilon
        )
        new = summed * old_scale * new_scale
        master[...] = new
        fast[block + 1, own_rows, :] = new.astype(BF)
        mine = fast.at[block + 1, own_rows]
        for peer in t_peers:
            remote(mine, mine, ag_send_sem.at[block], ag_sem.at[block], peer, h)

    def gather_finish(block):
        wait(fast.at[block + 1, 0 : 7 * shard], ag_sem.at[block])

    def query_pass(block):
        version = block + 1
        down = flip(fast[version, 2 * head : 3 * head, 0:head])
        gain = jnp.concatenate([gains[...], gains[...]], axis=1)
        for n in range(block_tokens // 256):
            span = slice(n * 256, (n + 1) * 256)
            q = queries[block, span]
            gate_pre = dot(q, fast[version, 0:head, 0:head])
            lift_pre = dot(q, fast[version, head : 2 * head, 0:head])
            hidden = (gate_pre * jax.nn.sigmoid(gate_pre) * lift_pre).astype(BF)
            out = dot_nt(down, hidden)
            out = out * lax.rsqrt(
                jnp.sum(out * out, axis=0, keepdims=True) * (1.0 / head) + epsilon
            )
            out_ref[block, :, span] = (out * gain).astype(BF)

    per_block = rounds // 2

    def step(s, carry):
        @pl.when(s + AHEAD < rounds)
        def _():
            send_own(s + AHEAD)

        @pl.when(s < rounds)
        def _():
            forward(s)

        @pl.when((s >= 1) & (s < rounds + 1))
        def _():
            forward_far(s - 1)

        c = s - LAG

        @pl.when(c >= 0)
        def _():
            wait(several(5), near_sem.at[c])
            wait(several(3), far_sem.at[c])
            half = c % HALVES
            u = c // HALVES
            project_keys(c)

            @pl.when(half == HALVES - 1)
            def _():
                finish_keys(u)

            @pl.when(c == per_block)
            def _():
                project_queries(0)

            @pl.when(c == per_block + 1)
            def _():
                reduce_finish(0)

            @pl.when(c == per_block + 3)
            def _():
                gather_finish(0)
                turn(1)

            first = jnp.where(c == per_block + 3, per, u)
            ready = (half == HALVES - 1) & (c != per_block + 1)
            lax.fori_loop(first, jnp.where(ready, u + 1, first), key_step, 0)

            @pl.when(c == per_block - 1)
            def _():
                reduce_send(0)

        return carry

    lax.fori_loop(0, rounds + LAG, step, 0)
    reduce_send(1)
    project_queries(1)
    query_pass(0)

    def drain(s, carry):
        wait(several(15), send_sem.at[s])
        return carry

    lax.fori_loop(0, rounds, drain, 0)
    wait(fast.at[1, 0 : 7 * shard], ag_send_sem.at[0])
    reduce_finish(1)
    gather_finish(1)
    query_pass(1)
    wait(fast.at[2, 0 : 7 * shard], ag_send_sem.at[1])


def local(codes, scales, w_qkv, w_rate, rate_bias, fast_gate, fast_lift, fast_down, out_gain):
    blocks, rows, depth = codes.shape
    head = fast_gate.shape[1]
    sources = lax.axis_size("tensor")
    shards = lax.axis_size("tokens")
    units = blocks * rows // UNIT
    rounds = units * HALVES
    tokens = sources * UNIT
    width = depth // HALVES
    factor = rate_base / math.sqrt(rows * sources * shards)
    stacked = 3 * head + PAD
    columns = w_qkv.shape[1] + w_rate.shape[1]
    vmem = pl.BlockSpec(memory_space=pltpu.VMEM)
    smem = pl.BlockSpec(memory_space=pltpu.SMEM)
    anyspace = pl.BlockSpec(memory_space=pl.ANY)
    dma = pltpu.SemaphoreType.DMA
    out = pl.pallas_call(
        functools.partial(kernel, factor),
        out_shape=jax.ShapeDtypeStruct((blocks, head, sources * rows), BF),
        in_specs=[anyspace, vmem, anyspace, anyspace, smem, vmem, vmem, vmem, vmem],
        out_specs=vmem,
        scratch_shapes=[
            pltpu.VMEM((blocks, HALVES, sources, rows, width), BF),
            pltpu.VMEM((columns, depth), BF),
            pltpu.VMEM((blocks * rows, depth), jnp.int32),
            pltpu.VMEM((scales.shape[2], depth), BF),
            pltpu.VMEM((blocks * rows, depth), F32),
            pltpu.VMEM((columns - head, tokens), F32),
            pltpu.VMEM((head, sources * rows), F32),
            pltpu.VMEM((stacked, KEYS), F32),
            pltpu.VMEM((stacked // shards, KEYS), F32),
            pltpu.VMEM((stacked, KEYS), BF),
            pltpu.VMEM((2, shards, stacked // shards, KEYS), BF),
            pltpu.VMEM((3, stacked, KEYS), BF),
            pltpu.VMEM((2, 2 * head, head), BF),
            pltpu.VMEM((head, 128), F32),
            pltpu.VMEM((blocks, sources * rows, head), BF),
            pltpu.VMEM((units, head, tokens), BF),
            pltpu.VMEM((units, head, tokens), BF),
            pltpu.VMEM((units, 8, tokens), F32),
            dma((3,)),
            dma((rounds,)),
            dma((rounds,)),
            dma((rounds,)),
            dma((rounds,)),
            dma((rounds,)),
            dma((rounds,)),
            dma((rounds,)),
            dma((2,)),
            dma((2,)),
            dma((2,)),
            dma((2,)),
        ],
        compiler_params=pltpu.CompilerParams(
            collective_id=0, has_side_effects=True, vmem_limit_bytes=58 << 20
        ),
        name="fast_weights",
    )(
        codes.reshape(blocks * rows, depth),
        scales.reshape(blocks * rows, scales.shape[2]),
        w_qkv.T,
        w_rate.T,
        rate_bias.reshape(1, 3),
        fast_gate,
        fast_lift,
        fast_down,
        out_gain,
    )
    return jnp.transpose(out, (0, 2, 1))


def solution(mesh):
    return jax.shard_map(
        local,
        mesh=mesh,
        in_specs=(
            P(None, ("tokens", "tensor"), None),
            P(None, ("tokens", "tensor"), None),
            P(None, "tensor"),
            P(),
            P("tensor"),
            P("tensor", None, None),
            P("tensor", None, None),
            P("tensor", None, None),
            P("tensor"),
        ),
        out_specs=P(None, "tokens", "tensor"),
        check_vma=False,
    )
```

```python
import functools
import math

import jax
import jax.numpy as jnp
from jax import lax
from jax.experimental import pallas as pl
from jax.experimental.pallas import tpu as pltpu
from jax.sharding import PartitionSpec as P

epsilon = 1e-06
rate_base = 0.15

MESH = pl.DeviceIdType.MESH
BF = jnp.bfloat16
F32 = jnp.float32

UNIT = 16
HALVES = 2
AHEAD = 1
LAG = 3
KEYS = 384
PAD = 64


def dot(a, b):
    return jnp.dot(a, b, preferred_element_type=F32)


def dot_nt(a, b):
    return lax.dot_general(a, b, (((1,), (1,)), ((), ())), preferred_element_type=F32)


def flip(a):
    return a.astype(F32).T.astype(BF)


def kernel(
    factor,
    codes_hbm,
    scales_ref,
    wqkv_hbm,
    wrate_hbm,
    bias_ref,
    gate_ref,
    lift_ref,
    down_ref,
    gain_ref,
    out_ref,
    acts,
    w,
    codes,
    spread,
    factors,
    kv_acc,
    q_acc,
    stack,
    master,
    rs_send,
    rs_recv,
    fast,
    gate_lift,
    gains,
    made,
    queries,
    keys,
    values,
    rates,
    local_sem,
    send_sem,
    z_sem,
    z2_sem,
    x_sem,
    a_sem,
    a2_sem,
    b_sem,
    b2_sem,
    near_sem,
    q_send_sem,
    q_sem,
    rs_send_sem,
    rs_sem,
    ag_send_sem,
    ag_sem,
):
    blocks, _, sources, rows_dev, width = acts.shape
    per = rows_dev // UNIT
    units = blocks * per
    rounds = units * HALVES
    part_a = width * 5 // 9 // 128 * 128
    middle = width // 256 * 128
    middle_a = part_a // 256 * 128
    depth = w.shape[1]
    head = gate_ref.shape[1]
    tokens = sources * UNIT
    block_tokens = sources * rows_dev
    chunk = 1280
    t = lax.axis_index("tokens")
    h = lax.axis_index("tensor")
    shards = 8
    z, hi, core = h // 4, (h // 2) % 2, h % 2

    def at(dz, other):
        side = 1 - hi if other else hi
        return lax.rem(z + dz, 4) * 4 + side * 2 + core

    up, down, across = at(1, False), at(3, False), at(2, False)
    x_peer, t_other = at(0, True), lax.rem(t + 4, shards)
    far_up, far_down, far_across = at(1, True), at(3, True), at(2, True)
    sibling = h + 1 - 2 * core
    t_peers = [lax.rem(t + k, shards) for k in range(1, shards)]

    barrier = pltpu.get_barrier_semaphore()
    for peer in (up, down, sibling):
        pl.semaphore_signal(barrier, inc=1, device_id=(t, peer), device_id_type=MESH)
    pl.semaphore_signal(barrier, inc=1, device_id=(t_other, x_peer), device_id_type=MESH)
    for peer in t_peers:
        pl.semaphore_signal(barrier, inc=1, device_id=(peer, h), device_id_type=MESH)

    codes_copy = pltpu.make_async_copy(codes_hbm, codes, local_sem.at[0])
    w_copy = pltpu.make_async_copy(wqkv_hbm, w.at[0 : 3 * head], local_sem.at[1])
    rate_copy = pltpu.make_async_copy(
        wrate_hbm, w.at[3 * head : w.shape[0]], local_sem.at[2]
    )
    codes_copy.start()
    w_copy.start()
    rate_copy.start()

    groups = scales_ref.shape[1]
    group = lax.broadcasted_iota(jnp.int32, (groups, depth), 0)
    column = lax.broadcasted_iota(jnp.int32, (groups, depth), 1)
    spread[...] = jnp.where(
        lax.shift_right_logical(column, 5) == group, 1.0, 0.0
    ).astype(BF)
    powers = lax.shift_left(jnp.ones_like(scales_ref[...]), scales_ref[...] - 119)
    powers = powers.astype(F32).astype(BF)
    step_n = 512

    def spread_step(n, carry):
        cols = pl.ds(pl.multiple_of(n * step_n, step_n), step_n)
        factors[:, cols] = dot(powers, spread[:, cols]) * (1.0 / 131072.0)
        return carry

    lax.fori_loop(0, depth // step_n, spread_step, 0)
    codes_copy.wait()

    def place(s):
        u = s // HALVES
        return u // per, s % HALVES, pl.ds(pl.multiple_of((u % per) * UNIT, UNIT), UNIT)

    def item(s, source):
        block, half, rows = place(s)
        return acts.at[block, half, source, rows]

    def decode(s, carry):
        block, half, unit_rows = place(s)
        rows = pl.ds(pl.multiple_of((s // HALVES) * UNIT, UNIT), UNIT)
        for n in range(width // step_n):
            start = half * width + n * step_n
            cols = pl.ds(pl.multiple_of(start, step_n), step_n)
            code = codes[rows, cols]
            lower = jnp.bitwise_and(code, 127)
            exponent = lax.shift_right_logical(lower, 3)
            mantissa = jnp.bitwise_and(lower, 7)
            normal = exponent > 0
            significand = jnp.where(normal, mantissa + 8, mantissa)
            significand = jnp.where(code >= 128, -significand, significand)
            shift = jnp.where(normal, exponent - 1, 0)
            whole = lax.shift_left(significand, shift).astype(F32)
            acts[block, half, h, unit_rows, n * step_n : (n + 1) * step_n] = (
                whole * factors[rows, cols]
            ).astype(BF)
        return carry

    def remote(src, dst, send, recv, tok, ten):
        pltpu.make_async_remote_copy(
            src_ref=src,
            dst_ref=dst,
            send_sem=send,
            recv_sem=recv,
            device_id=(tok, ten),
            device_id_type=MESH,
        ).start()

    def wait(ref, sem):
        pltpu.make_async_copy(ref, ref, sem).wait()

    def several(n, first=0, last=width):
        return acts.at[0, 0, 0:n, 0:UNIT, first:last]

    def move(s, source, first, last, sem, ten, tok=t):
        part = item(s, source)
        if last - first < width:
            part = part.at[:, first:last]
        remote(part, part, send_sem.at[s], sem.at[s], tok, ten)

    def share(s, source):
        move(s, source, 0, width, near_sem, sibling)

    def send_own(s):
        move(s, h, 0, width, z_sem, up)
        move(s, h, 0, width, z_sem, down)
        move(s, h, 0, width, x_sem, x_peer, t_other)
        share(s, h)

    def forward(s):
        wait(several(2), z_sem.at[s])
        move(s, down, 0, middle, z2_sem, up)
        move(s, up, middle, width, z2_sem, down)
        move(s, up, part_a, width, b_sem, x_peer, t_other)
        move(s, down, part_a, width, b_sem, x_peer, t_other)
        wait(several(1), x_sem.at[s])
        move(s, x_peer, 0, part_a, a_sem, up)
        move(s, x_peer, 0, part_a, a_sem, down)
        for source in (up, down, x_peer):
            share(s, source)

    def forward_second(s):
        wait(several(1), z2_sem.at[s])
        move(s, across, part_a, width, b2_sem, x_peer, t_other)
        wait(several(2, 0, part_a), a_sem.at[s])
        move(s, far_down, 0, middle_a, a2_sem, up)
        move(s, far_up, middle_a, part_a, a2_sem, down)
        wait(several(2, part_a, width), b_sem.at[s])
        for source in (across, far_up, far_down):
            share(s, source)

    def forward_third(s):
        wait(several(1, 0, part_a), a2_sem.at[s])
        wait(several(1, part_a, width), b2_sem.at[s])
        share(s, far_across)

    decode(0, 0)
    pl.semaphore_wait(barrier, 11)
    for s in range(AHEAD):
        if s > 0:
            decode(s, 0)
        send_own(s)
    lax.fori_loop(AHEAD, rounds, decode, 0)

    stack[...] = jnp.zeros_like(stack)
    stack[0:head, 0:head] = gate_ref[0]
    stack[head : 2 * head, 0:head] = lift_ref[0]
    stack[2 * head : 3 * head, 0:head] = down_ref[0]
    fast[0] = stack[...].astype(BF)
    shard = stack.shape[0] // shards
    own_rows = pl.ds(pl.multiple_of(t * shard, shard), shard)
    master[...] = stack[own_rows, :]
    stack[...] = jnp.zeros_like(stack)
    gains[...] = jnp.broadcast_to(gain_ref[...][None, :], (128, head)).T

    def turn(version):
        gate_lift[version, 0:head] = flip(fast[version, 0:head, 0:head])
        gate_lift[version, head : 2 * head] = flip(fast[version, head : 2 * head, 0:head])

    turn(0)
    w_copy.wait()
    rate_copy.wait()

    def project_keys(c):
        block, half, rows = place(c)

        def one(k, carry):
            cols = pl.ds(pl.multiple_of(k * chunk, chunk), chunk)
            deep = pl.ds(pl.multiple_of(half * width + k * chunk, chunk), chunk)
            x = acts[block, half, :, rows, cols].reshape(tokens, chunk)
            kv_acc[...] += dot_nt(w[head : w.shape[0], deep], x)
            return carry

        @pl.when(half == 0)
        def _():
            kv_acc[...] = jnp.zeros_like(kv_acc)

        lax.fori_loop(0, width // chunk, one, 0)

    def project_queries(c):
        block, half, rows = place(c)

        def one(k, carry):
            cols = pl.ds(pl.multiple_of(k * chunk, chunk), chunk)
            deep = pl.ds(pl.multiple_of(half * width + k * chunk, chunk), chunk)
            x = acts[block, half, :, rows, cols].reshape(tokens, chunk)
            q_acc[...] += dot_nt(w[0:head, deep], x)
            return carry

        @pl.when(half == 0)
        def _():
            q_acc[...] = jnp.zeros_like(q_acc)

        lax.fori_loop(0, width // chunk, one, 0)

    def finish_queries(u):
        block = u // per
        rows = pl.ds(pl.multiple_of((u % per) * UNIT, UNIT), UNIT)
        q = q_acc[...]
        q = q * lax.rsqrt(jnp.sum(q * q, axis=0, keepdims=True) * (1.0 / head) + epsilon)
        made[block, :, rows, 0:head] = q.T.astype(BF).reshape(sources, UNIT, head)
        for k in range(4):
            theirs = pl.ds(k * 4 + (1 - hi) * 2, 2)
            remote(
                made.at[block, theirs, rows],
                queries.at[block, theirs, rows],
                q_send_sem.at[u],
                q_sem.at[u],
                t_other,
                h,
            )
            mine = pl.ds(k * 4 + hi * 2, 2)
            queries[block, mine, rows] = made[block, mine, rows]

    def wait_queries(u):
        sample = queries.at[0, 0:8, 0:UNIT]
        wait(sample, q_sem.at[u])
        wait(sample, q_send_sem.at[u])

    def finish_keys(u):
        k = kv_acc[0:head]
        k = k * lax.rsqrt(jnp.sum(k * k, axis=0, keepdims=True) * (1.0 / head) + epsilon)
        keys[u] = k.astype(BF)
        values[u] = kv_acc[head : 2 * head].astype(BF)
        for i in range(3):
            logit = kv_acc[pl.ds(2 * head + 3 * h + i, 1), :] + bias_ref[0, i]
            soft = jnp.maximum(logit, 0.0) + jnp.log1p(jnp.exp(-jnp.abs(logit)))
            rates[u, i : i + 1] = soft * factor

    def key_step(u, carry):
        version = u // per
        kn = keys[u]
        v = values[u]
        pre = dot(gate_lift[version], kn)
        gate_pre = pre[0:head]
        lift_pre = pre[head : 2 * head]
        hidden_grad = dot(fast[version, 2 * head : 3 * head, 0:head], v)
        sig = jax.nn.sigmoid(gate_pre)
        activated = gate_pre * sig
        hidden = activated * lift_pre
        gate_grad = hidden_grad * lift_pre * (sig * (1.0 + gate_pre * (1.0 - sig)))
        lift_grad = hidden_grad * activated
        gate_grad = (gate_grad * rates[u, 0:1]).astype(BF)
        lift_grad = (lift_grad * rates[u, 1:2]).astype(BF)
        hidden = (hidden * rates[u, 2:3]).astype(BF)
        stack[0:head, 0:head] += dot_nt(kn, gate_grad)
        stack[head : 2 * head, 0:head] += dot_nt(kn, lift_grad)
        stack[2 * head : 3 * head, 0:head] += dot_nt(hidden, v)
        return carry

    def reduce_send(block):
        rs_send[...] = stack[...].astype(BF)
        for peer in t_peers:
            rows = pl.ds(pl.multiple_of(peer * shard, shard), shard)
            remote(
                rs_send.at[rows],
                rs_recv.at[block, t],
                rs_send_sem.at[block],
                rs_sem.at[block],
                peer,
                h,
            )
        rs_recv[block, t] = rs_send[own_rows, :]
        stack[...] = jnp.zeros_like(stack)

    def reduce_finish(block):
        wait(rs_recv.at[block, 0:7], rs_sem.at[block])
        wait(rs_send.at[0 : 7 * shard], rs_send_sem.at[block])
        summed = rs_recv[block, 0].astype(F32)
        for j in range(1, shards):
            summed = summed + rs_recv[block, j].astype(F32)
        old = master[...]
        summed = old + summed
        old_scale = jnp.sqrt(
            jnp.sum(old * old, axis=1, keepdims=True) * (1.0 / head) + epsilon
        )
        new_scale = lax.rsqrt(
            jnp.sum(summed * summed, axis=1, keepdims=True) * (1.0 / head) + epsilon
        )
        new = summed * old_scale * new_scale
        master[...] = new
        fast[block + 1, own_rows, :] = new.astype(BF)
        mine = fast.at[block + 1, own_rows]
        for peer in t_peers:
            remote(mine, mine, ag_send_sem.at[block], ag_sem.at[block], peer, h)

    def gather_finish(block):
        wait(fast.at[block + 1, 0 : 7 * shard], ag_sem.at[block])

    def query_pass(block):
        version = block + 1
        down = flip(fast[version, 2 * head : 3 * head, 0:head])
        gain = jnp.concatenate([gains[...], gains[...]], axis=1)
        for j in range(per):
            wait_queries(block * per + j)
        flat = queries[block].reshape(block_tokens, KEYS)
        for n in range(block_tokens // 256):
            span = slice(n * 256, (n + 1) * 256)
            q = flat[span, 0:head]
            gate_pre = dot(q, fast[version, 0:head, 0:head])
            lift_pre = dot(q, fast[version, head : 2 * head, 0:head])
            hidden = (gate_pre * jax.nn.sigmoid(gate_pre) * lift_pre).astype(BF)
            out = dot_nt(down, hidden)
            out = out * lax.rsqrt(
                jnp.sum(out * out, axis=0, keepdims=True) * (1.0 / head) + epsilon
            )
            out_ref[block, :, span] = (out * gain).astype(BF)

    per_block = rounds // 2

    def step(s, carry):
        @pl.when(s + AHEAD < rounds)
        def _():
            send_own(s + AHEAD)

        @pl.when(s < rounds)
        def _():
            forward(s)

        @pl.when((s >= 1) & (s < rounds + 1))
        def _():
            forward_second(s - 1)

        @pl.when((s >= 2) & (s < rounds + 2))
        def _():
            forward_third(s - 2)

        c = s - LAG

        @pl.when(c >= 0)
        def _():
            wait(several(8), near_sem.at[c])
            half = c % HALVES
            u = c // HALVES
            project_keys(c)

            @pl.when(half == HALVES - 1)
            def _():
                finish_keys(u)

            @pl.when(c == per_block + 1)
            def _():
                reduce_finish(0)

            @pl.when(c == per_block + 3)
            def _():
                gather_finish(0)
                turn(1)

            first = jnp.where(c == per_block + 3, per, u)
            ready = (half == HALVES - 1) & (c != per_block + 1)
            lax.fori_loop(first, jnp.where(ready, u + 1, first), key_step, 0)

            @pl.when(c == per_block - 1)
            def _():
                reduce_send(0)

            @pl.when(c < rounds - HALVES)
            def _():
                project_queries(c)

                @pl.when(half == HALVES - 1)
                def _():
                    finish_queries(u)

        return carry

    lax.fori_loop(0, rounds + LAG, step, 0)
    reduce_send(1)
    for half in range(HALVES):
        project_queries(rounds - HALVES + half)
    finish_queries(units - 1)
    query_pass(0)

    def drain(s, carry):
        wait(several(15), send_sem.at[s])
        return carry

    lax.fori_loop(0, rounds, drain, 0)
    wait(fast.at[1, 0 : 7 * shard], ag_send_sem.at[0])
    reduce_finish(1)
    gather_finish(1)
    query_pass(1)
    wait(fast.at[2, 0 : 7 * shard], ag_send_sem.at[1])


def local(codes, scales, w_qkv, w_rate, rate_bias, fast_gate, fast_lift, fast_down, out_gain):
    blocks, rows, depth = codes.shape
    head = fast_gate.shape[1]
    sources = lax.axis_size("tensor")
    shards = lax.axis_size("tokens")
    units = blocks * rows // UNIT
    rounds = units * HALVES
    tokens = sources * UNIT
    width = depth // HALVES
    factor = rate_base / math.sqrt(rows * sources * shards)
    stacked = 3 * head + PAD
    columns = w_qkv.shape[1] + w_rate.shape[1]
    vmem = pl.BlockSpec(memory_space=pltpu.VMEM)
    smem = pl.BlockSpec(memory_space=pltpu.SMEM)
    anyspace = pl.BlockSpec(memory_space=pl.ANY)
    dma = pltpu.SemaphoreType.DMA
    out = pl.pallas_call(
        functools.partial(kernel, factor),
        out_shape=jax.ShapeDtypeStruct((blocks, head, sources * rows), BF),
        in_specs=[anyspace, vmem, anyspace, anyspace, smem, vmem, vmem, vmem, vmem],
        out_specs=vmem,
        scratch_shapes=[
            pltpu.VMEM((blocks, HALVES, sources, rows, width), BF),
            pltpu.VMEM((columns, depth), BF),
            pltpu.VMEM((blocks * rows, depth), jnp.int32),
            pltpu.VMEM((scales.shape[2], depth), BF),
            pltpu.VMEM((blocks * rows, depth), F32),
            pltpu.VMEM((columns - head, tokens), F32),
            pltpu.VMEM((head, tokens), F32),
            pltpu.VMEM((stacked, KEYS), F32),
            pltpu.VMEM((stacked // shards, KEYS), F32),
            pltpu.VMEM((stacked, KEYS), BF),
            pltpu.VMEM((2, shards, stacked // shards, KEYS), BF),
            pltpu.VMEM((3, stacked, KEYS), BF),
            pltpu.VMEM((2, 2 * head, head), BF),
            pltpu.VMEM((head, 128), F32),
            pltpu.VMEM((blocks, sources, rows, KEYS), BF),
            pltpu.VMEM((blocks, sources, rows, KEYS), BF),
            pltpu.VMEM((units, head, tokens), BF),
            pltpu.VMEM((units, head, tokens), BF),
            pltpu.VMEM((units, 8, tokens), F32),
            dma((3,)),
            dma((rounds,)),
            dma((rounds,)),
            dma((rounds,)),
            dma((rounds,)),
            dma((rounds,)),
            dma((rounds,)),
            dma((rounds,)),
            dma((rounds,)),
            dma((rounds,)),
            dma((units,)),
            dma((units,)),
            dma((2,)),
            dma((2,)),
            dma((2,)),
            dma((2,)),
        ],
        compiler_params=pltpu.CompilerParams(
            collective_id=0, has_side_effects=True, vmem_limit_bytes=58 << 20
        ),
        name="fast_weights",
    )(
        codes.reshape(blocks * rows, depth),
        scales.reshape(blocks * rows, scales.shape[2]),
        w_qkv.T,
        w_rate.T,
        rate_bias.reshape(1, 3),
        fast_gate,
        fast_lift,
        fast_down,
        out_gain,
    )
    return jnp.transpose(out, (0, 2, 1))


def solution(mesh):
    return jax.shard_map(
        local,
        mesh=mesh,
        in_specs=(
            P(None, ("tokens", "tensor"), None),
            P(None, ("tokens", "tensor"), None),
            P(None, "tensor"),
            P(),
            P("tensor"),
            P("tensor", None, None),
            P("tensor", None, None),
            P("tensor", None, None),
            P("tensor"),
        ),
        out_specs=P(None, "tokens", "tensor"),
        check_vma=False,
    )
```

```python
import functools
import math

import jax
import jax.numpy as jnp
from jax import lax
from jax.experimental import pallas as pl
from jax.experimental.pallas import tpu as pltpu
from jax.sharding import PartitionSpec as P

epsilon = 1e-06
rate_base = 0.15

MESH = pl.DeviceIdType.MESH
BF = jnp.bfloat16
F32 = jnp.float32

UNIT = 16
HALVES = 2
AHEAD = 1
LAG = 4
KEYS = 384
SUB = 64
PAD = 64


def dot(a, b):
    return jnp.dot(a, b, preferred_element_type=F32)


def dot_nt(a, b):
    return lax.dot_general(a, b, (((1,), (1,)), ((), ())), preferred_element_type=F32)


def flip(a):
    return a.astype(F32).T.astype(BF)


def kernel(
    factor,
    codes_hbm,
    scales_ref,
    wqkv_hbm,
    wrate_hbm,
    bias_ref,
    gate_ref,
    lift_ref,
    down_ref,
    gain_ref,
    out_ref,
    acts,
    w,
    codes,
    spread,
    factors,
    kv_acc,
    q_acc,
    stack,
    master,
    rs_send,
    rs_recv,
    gathered,
    first_weights,
    fast,
    gate_lift,
    gains,
    made,
    queries,
    keys,
    values,
    rates,
    local_sem,
    send_sem,
    z_sem,
    z2_sem,
    x_sem,
    a_sem,
    a2_sem,
    b_sem,
    b2_sem,
    near_sem,
    q_send_sem,
    q_sem,
    rs_send_sem,
    rs_sem,
    ag_send_sem,
    ag_sem,
):
    blocks, _, sources, rows_dev, width = acts.shape
    per = rows_dev // UNIT
    units = blocks * per
    rounds = units * HALVES
    part_a = width * 5 // 9 // 128 * 128
    middle = width // 256 * 128
    middle_a = part_a // 256 * 128
    depth = w.shape[1]
    head = gate_ref.shape[1]
    tokens = sources * UNIT
    block_tokens = sources * rows_dev
    chunk = 1280
    t = lax.axis_index("tokens")
    h = lax.axis_index("tensor")
    shards = 8
    z, hi, core = h // 4, (h // 2) % 2, h % 2

    def at(dz, other):
        side = 1 - hi if other else hi
        return lax.rem(z + dz, 4) * 4 + side * 2 + core

    up, down, across = at(1, False), at(3, False), at(2, False)
    x_peer, t_other = at(0, True), lax.rem(t + 4, shards)
    far_up, far_down, far_across = at(1, True), at(3, True), at(2, True)
    sibling = h + 1 - 2 * core
    t_peers = [lax.rem(t + k, shards) for k in range(1, shards)]

    barrier = pltpu.get_barrier_semaphore()
    for peer in (up, down, sibling):
        pl.semaphore_signal(barrier, inc=1, device_id=(t, peer), device_id_type=MESH)
    pl.semaphore_signal(barrier, inc=1, device_id=(t_other, x_peer), device_id_type=MESH)
    for peer in t_peers:
        pl.semaphore_signal(barrier, inc=1, device_id=(peer, h), device_id_type=MESH)

    codes_copy = pltpu.make_async_copy(codes_hbm, codes, local_sem.at[0])
    w_copy = pltpu.make_async_copy(wqkv_hbm, w.at[0 : 3 * head], local_sem.at[1])
    rate_copy = pltpu.make_async_copy(
        wrate_hbm, w.at[3 * head : w.shape[0]], local_sem.at[2]
    )
    codes_copy.start()
    fast_copies = [
        pltpu.make_async_copy(ref, first_weights.at[i], local_sem.at[3 + i])
        for i, ref in enumerate((gate_ref, lift_ref, down_ref))
    ]
    for copy in fast_copies:
        copy.start()
    w_copy.start()
    rate_copy.start()

    groups = scales_ref.shape[1]
    group = lax.broadcasted_iota(jnp.int32, (groups, depth), 0)
    column = lax.broadcasted_iota(jnp.int32, (groups, depth), 1)
    spread[...] = jnp.where(
        lax.shift_right_logical(column, 5) == group, 1.0, 0.0
    ).astype(BF)
    powers = lax.shift_left(jnp.ones_like(scales_ref[...]), scales_ref[...] - 119)
    powers = powers.astype(F32).astype(BF)
    step_n = 512

    def spread_step(n, carry):
        cols = pl.ds(pl.multiple_of(n * step_n, step_n), step_n)
        factors[:, cols] = dot(powers, spread[:, cols]) * (1.0 / 131072.0)
        return carry

    lax.fori_loop(0, depth // step_n, spread_step, 0)
    codes_copy.wait()

    def place(s):
        u = s // HALVES
        return u // per, s % HALVES, pl.ds(pl.multiple_of((u % per) * UNIT, UNIT), UNIT)

    def item(s, source):
        block, half, rows = place(s)
        return acts.at[block, half, source, rows]

    def decode(s, carry):
        block, half, unit_rows = place(s)
        rows = pl.ds(pl.multiple_of((s // HALVES) * UNIT, UNIT), UNIT)
        for n in range(width // step_n):
            start = half * width + n * step_n
            cols = pl.ds(pl.multiple_of(start, step_n), step_n)
            code = codes[rows, cols]
            lower = jnp.bitwise_and(code, 127)
            exponent = lax.shift_right_logical(lower, 3)
            mantissa = jnp.bitwise_and(lower, 7)
            normal = exponent > 0
            significand = jnp.where(normal, mantissa + 8, mantissa)
            significand = jnp.where(code >= 128, -significand, significand)
            shift = jnp.where(normal, exponent - 1, 0)
            whole = lax.shift_left(significand, shift).astype(F32)
            acts[block, half, h, unit_rows, n * step_n : (n + 1) * step_n] = (
                whole * factors[rows, cols]
            ).astype(BF)
        return carry

    def remote(src, dst, send, recv, tok, ten):
        pltpu.make_async_remote_copy(
            src_ref=src,
            dst_ref=dst,
            send_sem=send,
            recv_sem=recv,
            device_id=(tok, ten),
            device_id_type=MESH,
        ).start()

    def wait(ref, sem):
        pltpu.make_async_copy(ref, ref, sem).wait()

    def several(n, first=0, last=width):
        return acts.at[0, 0, 0:n, 0:UNIT, first:last]

    def move(s, source, first, last, sem, ten, tok=t):
        part = item(s, source)
        if last - first < width:
            part = part.at[:, first:last]
        remote(part, part, send_sem.at[s], sem.at[s], tok, ten)

    def share(s, source):
        move(s, source, 0, width, near_sem, sibling)

    def send_own(s):
        move(s, h, 0, width, z_sem, up)
        move(s, h, 0, width, z_sem, down)
        move(s, h, 0, width, x_sem, x_peer, t_other)
        share(s, h)

    def forward(s):
        wait(several(2), z_sem.at[s])
        move(s, down, 0, middle, z2_sem, up)
        move(s, up, middle, width, z2_sem, down)
        move(s, up, part_a, width, b_sem, x_peer, t_other)
        move(s, down, part_a, width, b_sem, x_peer, t_other)
        wait(several(1), x_sem.at[s])
        move(s, x_peer, 0, part_a, a_sem, up)
        move(s, x_peer, 0, part_a, a_sem, down)
        for source in (up, down, x_peer):
            share(s, source)

    def forward_second(s):
        wait(several(1), z2_sem.at[s])
        move(s, across, part_a, width, b2_sem, x_peer, t_other)
        wait(several(2, 0, part_a), a_sem.at[s])
        move(s, far_down, 0, middle_a, a2_sem, up)
        move(s, far_up, middle_a, part_a, a2_sem, down)
        wait(several(2, part_a, width), b_sem.at[s])
        for source in (across, far_up, far_down):
            share(s, source)

    def forward_third(s):
        wait(several(1, 0, part_a), a2_sem.at[s])
        wait(several(1, part_a, width), b2_sem.at[s])
        share(s, far_across)

    decode(0, 0)
    pl.semaphore_wait(barrier, 11)
    for s in range(AHEAD):
        if s > 0:
            decode(s, 0)
        send_own(s)

    stack[...] = jnp.zeros_like(stack)
    for i, copy in enumerate(fast_copies):
        copy.wait()
        stack[i * head : (i + 1) * head, 0:head] = first_weights[i, 0]
    fast[0] = stack[...].astype(BF)
    for part in range(2):
        own_rows = pl.ds(pl.multiple_of((part * shards + t) * SUB, SUB), SUB)
        master[part] = stack[own_rows, 0:head]
    stack[...] = jnp.zeros_like(stack)
    gains[...] = jnp.broadcast_to(gain_ref[...][None, :], (128, head)).T

    def turn(version):
        gate_lift[version, 0:head] = flip(fast[version, 0:head, 0:head])
        gate_lift[version, head : 2 * head] = flip(fast[version, head : 2 * head, 0:head])

    turn(0)
    w_copy.wait()
    rate_copy.wait()

    def project_keys(c):
        block, half, rows = place(c)

        def one(k, carry):
            cols = pl.ds(pl.multiple_of(k * chunk, chunk), chunk)
            deep = pl.ds(pl.multiple_of(half * width + k * chunk, chunk), chunk)
            x = acts[block, half, :, rows, cols].reshape(tokens, chunk)
            kv_acc[...] += dot_nt(w[head : w.shape[0], deep], x)
            return carry

        @pl.when(half == 0)
        def _():
            kv_acc[...] = jnp.zeros_like(kv_acc)

        lax.fori_loop(0, width // chunk, one, 0)

    def project_queries(c):
        block, half, rows = place(c)

        def one(k, carry):
            cols = pl.ds(pl.multiple_of(k * chunk, chunk), chunk)
            deep = pl.ds(pl.multiple_of(half * width + k * chunk, chunk), chunk)
            x = acts[block, half, :, rows, cols].reshape(tokens, chunk)
            q_acc[...] += dot_nt(w[0:head, deep], x)
            return carry

        @pl.when(half == 0)
        def _():
            q_acc[...] = jnp.zeros_like(q_acc)

        lax.fori_loop(0, width // chunk, one, 0)

    def finish_queries(u):
        block = u // per
        rows = pl.ds(pl.multiple_of((u % per) * UNIT, UNIT), UNIT)
        q = q_acc[...]
        q = q * lax.rsqrt(jnp.sum(q * q, axis=0, keepdims=True) * (1.0 / head) + epsilon)
        made[block, :, rows, 0:head] = q.T.astype(BF).reshape(sources, UNIT, head)
        for k in range(4):
            theirs = pl.ds(k * 4 + (1 - hi) * 2, 2)
            remote(
                made.at[block, theirs, rows],
                queries.at[block, theirs, rows],
                q_send_sem.at[u],
                q_sem.at[u],
                t_other,
                h,
            )
            mine = pl.ds(k * 4 + hi * 2, 2)
            queries[block, mine, rows] = made[block, mine, rows]

    def wait_queries(u):
        sample = queries.at[0, 0:8, 0:UNIT]
        wait(sample, q_sem.at[u])
        wait(sample, q_send_sem.at[u])

    def finish_keys(u):
        k = kv_acc[0:head]
        k = k * lax.rsqrt(jnp.sum(k * k, axis=0, keepdims=True) * (1.0 / head) + epsilon)
        keys[u] = k.astype(BF)
        values[u] = kv_acc[head : 2 * head].astype(BF)
        for i in range(3):
            logit = kv_acc[pl.ds(2 * head + 3 * h + i, 1), :] + bias_ref[0, i]
            soft = jnp.maximum(logit, 0.0) + jnp.log1p(jnp.exp(-jnp.abs(logit)))
            rates[u, i : i + 1] = soft * factor

    def key_step(u, carry):
        version = u // per
        kn = keys[u]
        v = values[u]
        pre = dot(gate_lift[version], kn)
        gate_pre = pre[0:head]
        lift_pre = pre[head : 2 * head]
        hidden_grad = dot(fast[version, 2 * head : 3 * head, 0:head], v)
        sig = jax.nn.sigmoid(gate_pre)
        activated = gate_pre * sig
        hidden = activated * lift_pre
        gate_grad = hidden_grad * lift_pre * (sig * (1.0 + gate_pre * (1.0 - sig)))
        lift_grad = hidden_grad * activated
        gate_grad = (gate_grad * rates[u, 0:1]).astype(BF)
        lift_grad = (lift_grad * rates[u, 1:2]).astype(BF)
        hidden = (hidden * rates[u, 2:3]).astype(BF)
        stack[0:head, 0:head] += dot_nt(kn, gate_grad)
        stack[head : 2 * head, 0:head] += dot_nt(kn, lift_grad)
        stack[2 * head : 3 * head, 0:head] += dot_nt(hidden, v)
        return carry

    def pack(x):
        third = jnp.concatenate(
            [x[0 : SUB // 2, 256 : 256 + PAD], x[SUB // 2 : SUB, 256 : 256 + PAD]], axis=1
        )
        return jnp.concatenate([x[:, 0:128], x[:, 128:256], third], axis=0).astype(BF)

    def unpack(p):
        p = p.astype(F32)
        third = p[2 * SUB : 2 * SUB + SUB // 2]
        third = jnp.concatenate([third[:, 0:PAD], third[:, PAD : 2 * PAD]], axis=0)
        return jnp.concatenate([p[0:SUB], p[SUB : 2 * SUB], third], axis=1)

    def reduce_send(block):
        for part in range(2):

            def pack_one(j, carry, part=part):
                rows = pl.ds(pl.multiple_of((part * shards + j) * SUB, SUB), SUB)
                rs_send[part, j] = pack(stack[rows, :])
                return carry

            lax.fori_loop(0, shards, pack_one, 0)
            for peer in t_peers:
                remote(
                    rs_send.at[part, peer],
                    rs_recv.at[block, part, t],
                    rs_send_sem.at[block, part],
                    rs_sem.at[block, part],
                    peer,
                    h,
                )
            rs_recv[block, part, t] = rs_send[part, t]
        stack[...] = jnp.zeros_like(stack)

    def reduce_finish(block, part):
        wait(rs_recv.at[block, part, 0:7], rs_sem.at[block, part])
        wait(rs_send.at[part, 0:7], rs_send_sem.at[block, part])
        summed = rs_recv[block, part, 0].astype(F32)
        for j in range(1, shards):
            summed = summed + rs_recv[block, part, j].astype(F32)
        old = master[part]
        summed = old + unpack(summed)
        old_scale = jnp.sqrt(
            jnp.sum(old * old, axis=1, keepdims=True) * (1.0 / head) + epsilon
        )
        new_scale = lax.rsqrt(
            jnp.sum(summed * summed, axis=1, keepdims=True) * (1.0 / head) + epsilon
        )
        new = summed * old_scale * new_scale
        master[part] = new
        gathered[block, part, t] = pack(new)
        mine = gathered.at[block, part, t]
        for peer in t_peers:
            remote(
                mine, mine, ag_send_sem.at[block, part], ag_sem.at[block, part], peer, h
            )

    def gather_finish(block):
        for part in range(2):
            wait(gathered.at[block, part, 0:7], ag_sem.at[block, part])

            def unpack_one(j, carry, part=part):
                rows = pl.ds(pl.multiple_of((part * shards + j) * SUB, SUB), SUB)
                fast[block + 1, rows, 0:head] = unpack(gathered[block, part, j]).astype(BF)
                return carry

            lax.fori_loop(0, shards, unpack_one, 0)

    def gather_drain(block):
        for part in range(2):
            wait(gathered.at[block, part, 0:7], ag_send_sem.at[block, part])

    def query_pass(block):
        version = block + 1
        down = flip(fast[version, 2 * head : 3 * head, 0:head])
        gain = jnp.concatenate([gains[...], gains[...]], axis=1)
        for j in range(per):
            wait_queries(block * per + j)
        flat = queries[block].reshape(block_tokens, KEYS)
        for n in range(block_tokens // 256):
            span = slice(n * 256, (n + 1) * 256)
            q = flat[span, 0:head]
            gate_pre = dot(q, fast[version, 0:head, 0:head])
            lift_pre = dot(q, fast[version, head : 2 * head, 0:head])
            hidden = (gate_pre * jax.nn.sigmoid(gate_pre) * lift_pre).astype(BF)
            out = dot_nt(down, hidden)
            out = out * lax.rsqrt(
                jnp.sum(out * out, axis=0, keepdims=True) * (1.0 / head) + epsilon
            )
            out_ref[block, :, span] = (out * gain).astype(BF)

    per_block = rounds // 2

    def step(s, carry):
        @pl.when(s + AHEAD < rounds)
        def _():
            decode(s + AHEAD, 0)
            send_own(s + AHEAD)

        @pl.when(s < rounds)
        def _():
            forward(s)

        c = s - LAG
        half = c % HALVES
        u = c // HALVES

        @pl.when(c >= 0)
        def _():
            wait(several(8), near_sem.at[c])
            project_keys(c)

        @pl.when((s >= 1) & (s < rounds + 1))
        def _():
            forward_second(s - 1)

        @pl.when((c >= 0) & (c < rounds - HALVES))
        def _():
            project_queries(c)

            @pl.when(half == HALVES - 1)
            def _():
                finish_queries(u)

        @pl.when((c >= 0) & (half == HALVES - 1))
        def _():
            finish_keys(u)

        @pl.when((s >= 2) & (s < rounds + 2))
        def _():
            forward_third(s - 2)

        @pl.when(c == per_block + 1)
        def _():
            reduce_finish(0, 0)
            reduce_finish(0, 1)

        @pl.when(c == per_block + 3)
        def _():
            gather_finish(0)
            turn(1)

        first = jnp.where(c == per_block + 3, per, u)
        ready = (c >= 0) & (half == HALVES - 1) & (c != per_block + 1)
        lax.fori_loop(first, jnp.where(ready, u + 1, first), key_step, 0)

        @pl.when(c == per_block - 1)
        def _():
            reduce_send(0)

        return carry

    lax.fori_loop(0, rounds + LAG, step, 0)
    reduce_send(1)
    for half in range(HALVES):
        project_queries(rounds - HALVES + half)
    finish_queries(units - 1)
    gather_drain(0)
    reduce_finish(1, 0)
    reduce_finish(1, 1)
    query_pass(0)

    def drain(s, carry):
        wait(several(15), send_sem.at[s])
        return carry

    lax.fori_loop(0, rounds, drain, 0)
    gather_finish(1)
    query_pass(1)
    gather_drain(1)


def local(codes, scales, w_qkv, w_rate, rate_bias, fast_gate, fast_lift, fast_down, out_gain):
    blocks, rows, depth = codes.shape
    head = fast_gate.shape[1]
    sources = lax.axis_size("tensor")
    shards = lax.axis_size("tokens")
    units = blocks * rows // UNIT
    rounds = units * HALVES
    tokens = sources * UNIT
    width = depth // HALVES
    factor = rate_base / math.sqrt(rows * sources * shards)
    stacked = 3 * head + PAD
    columns = w_qkv.shape[1] + w_rate.shape[1]
    vmem = pl.BlockSpec(memory_space=pltpu.VMEM)
    smem = pl.BlockSpec(memory_space=pltpu.SMEM)
    anyspace = pl.BlockSpec(memory_space=pl.ANY)
    dma = pltpu.SemaphoreType.DMA
    out = pl.pallas_call(
        functools.partial(kernel, factor),
        out_shape=jax.ShapeDtypeStruct((blocks, head, sources * rows), BF),
        in_specs=[anyspace, vmem, anyspace, anyspace, smem] + [anyspace] * 3 + [vmem],
        out_specs=vmem,
        scratch_shapes=[
            pltpu.VMEM((blocks, HALVES, sources, rows, width), BF),
            pltpu.VMEM((columns, depth), BF),
            pltpu.VMEM((blocks * rows, depth), jnp.int32),
            pltpu.VMEM((scales.shape[2], depth), BF),
            pltpu.VMEM((blocks * rows, depth), F32),
            pltpu.VMEM((columns - head, tokens), F32),
            pltpu.VMEM((head, tokens), F32),
            pltpu.VMEM((stacked, KEYS), F32),
            pltpu.VMEM((2, SUB, head), F32),
            pltpu.VMEM((2, shards, SUB * 5 // 2, 128), BF),
            pltpu.VMEM((2, 2, shards, SUB * 5 // 2, 128), BF),
            pltpu.VMEM((2, 2, shards, SUB * 5 // 2, 128), BF),
            pltpu.VMEM((3, 1, head, head), F32),
            pltpu.VMEM((3, stacked, KEYS), BF),
            pltpu.VMEM((2, 2 * head, head), BF),
            pltpu.VMEM((head, 128), F32),
            pltpu.VMEM((blocks, sources, rows, KEYS), BF),
            pltpu.VMEM((blocks, sources, rows, KEYS), BF),
            pltpu.VMEM((units, head, tokens), BF),
            pltpu.VMEM((units, head, tokens), BF),
            pltpu.VMEM((units, 8, tokens), F32),
            dma((6,)),
            dma((rounds,)),
            dma((rounds,)),
            dma((rounds,)),
            dma((rounds,)),
            dma((rounds,)),
            dma((rounds,)),
            dma((rounds,)),
            dma((rounds,)),
            dma((rounds,)),
            dma((units,)),
            dma((units,)),
            dma((2, 2)),
            dma((2, 2)),
            dma((2, 2)),
            dma((2, 2)),
        ],
        compiler_params=pltpu.CompilerParams(
            collective_id=0, has_side_effects=True, vmem_limit_bytes=58 << 20
        ),
        name="fast_weights",
    )(
        codes.reshape(blocks * rows, depth),
        scales.reshape(blocks * rows, scales.shape[2]),
        w_qkv.T,
        w_rate.T,
        rate_bias.reshape(1, 3),
        fast_gate,
        fast_lift,
        fast_down,
        out_gain,
    )
    return jnp.transpose(out, (0, 2, 1))


def solution(mesh):
    return jax.shard_map(
        local,
        mesh=mesh,
        in_specs=(
            P(None, ("tokens", "tensor"), None),
            P(None, ("tokens", "tensor"), None),
            P(None, "tensor"),
            P(),
            P("tensor"),
            P("tensor", None, None),
            P("tensor", None, None),
            P("tensor", None, None),
            P("tensor"),
        ),
        out_specs=P(None, "tokens", "tensor"),
        check_vma=False,
    )
```

```python
import functools
import math

import jax
import jax.numpy as jnp
from jax import lax
from jax.experimental import pallas as pl
from jax.experimental.pallas import tpu as pltpu
from jax.sharding import PartitionSpec as P

epsilon = 1e-06
rate_base = 0.15

MESH = pl.DeviceIdType.MESH
BF = jnp.bfloat16
F32 = jnp.float32

UNIT = 16
HALVES = 2
AHEAD = 1
LAG = 3
KEYS = 384
SUB = 64
PAD = 64


def dot(a, b):
    return jnp.dot(a, b, preferred_element_type=F32)


def dot_nt(a, b):
    return lax.dot_general(a, b, (((1,), (1,)), ((), ())), preferred_element_type=F32)


def flip(a):
    return a.astype(F32).T.astype(BF)


def kernel(
    factor,
    codes_hbm,
    scales_ref,
    wqkv_hbm,
    wrate_hbm,
    bias_ref,
    gate_ref,
    lift_ref,
    down_ref,
    gain_ref,
    out_ref,
    acts,
    w,
    codes,
    spread,
    factors,
    kv_acc,
    q_acc,
    stack,
    master,
    rs_send,
    rs_recv,
    gathered,
    first_weights,
    fast,
    gate_lift,
    gains,
    made,
    queries,
    keys,
    values,
    rates,
    local_sem,
    send_sem,
    z_sem,
    z2_sem,
    x_sem,
    a_sem,
    a2_sem,
    b_sem,
    b2_sem,
    near_sem,
    q_send_sem,
    q_sem,
    rs_send_sem,
    rs_sem,
    ag_send_sem,
    ag_sem,
):
    blocks, _, sources, rows_dev, width = acts.shape
    per = rows_dev // UNIT
    units = blocks * per
    rounds = units * HALVES
    part_a = width * 5 // 9 // 128 * 128
    middle = width // 256 * 128
    middle_a = part_a // 256 * 128
    depth = w.shape[1]
    head = gate_ref.shape[1]
    tokens = sources * UNIT
    block_tokens = sources * rows_dev
    chunk = 1280
    t = lax.axis_index("tokens")
    h = lax.axis_index("tensor")
    shards = 8
    z, hi, core = h // 4, (h // 2) % 2, h % 2

    def at(dz, other):
        side = 1 - hi if other else hi
        return lax.rem(z + dz, 4) * 4 + side * 2 + core

    up, down, across = at(1, False), at(3, False), at(2, False)
    x_peer, t_other = at(0, True), lax.rem(t + 4, shards)
    far_up, far_down, far_across = at(1, True), at(3, True), at(2, True)
    sibling = h + 1 - 2 * core
    t_peers = [lax.rem(t + k, shards) for k in range(1, shards)]

    barrier = pltpu.get_barrier_semaphore()
    for peer in (up, down, sibling):
        pl.semaphore_signal(barrier, inc=1, device_id=(t, peer), device_id_type=MESH)
    pl.semaphore_signal(barrier, inc=1, device_id=(t_other, x_peer), device_id_type=MESH)
    for peer in t_peers:
        pl.semaphore_signal(barrier, inc=1, device_id=(peer, h), device_id_type=MESH)

    codes_copy = pltpu.make_async_copy(codes_hbm, codes, local_sem.at[0])
    w_copy = pltpu.make_async_copy(wqkv_hbm, w.at[0 : 3 * head], local_sem.at[1])
    rate_copy = pltpu.make_async_copy(
        wrate_hbm, w.at[3 * head : w.shape[0]], local_sem.at[2]
    )
    codes_copy.start()
    fast_copies = [
        pltpu.make_async_copy(ref, first_weights.at[i], local_sem.at[3 + i])
        for i, ref in enumerate((gate_ref, lift_ref, down_ref))
    ]
    for copy in fast_copies:
        copy.start()
    w_copy.start()
    rate_copy.start()

    groups = scales_ref.shape[1]
    group = lax.broadcasted_iota(jnp.int32, (groups, depth), 0)
    column = lax.broadcasted_iota(jnp.int32, (groups, depth), 1)
    spread[...] = jnp.where(
        lax.shift_right_logical(column, 5) == group, 1.0, 0.0
    ).astype(BF)
    powers = lax.shift_left(jnp.ones_like(scales_ref[...]), scales_ref[...] - 119)
    powers = powers.astype(F32).astype(BF)
    step_n = 512

    def spread_step(n, carry):
        cols = pl.ds(pl.multiple_of(n * step_n, step_n), step_n)
        factors[:, cols] = dot(powers, spread[:, cols]) * (1.0 / 131072.0)
        return carry

    lax.fori_loop(0, depth // step_n, spread_step, 0)
    codes_copy.wait()

    def place(s):
        u = s // HALVES
        return u // per, s % HALVES, pl.ds(pl.multiple_of((u % per) * UNIT, UNIT), UNIT)

    def item(s, source):
        block, half, rows = place(s)
        return acts.at[block, half, source, rows]

    def decode(s, carry):
        block, half, unit_rows = place(s)
        rows = pl.ds(pl.multiple_of((s // HALVES) * UNIT, UNIT), UNIT)
        for n in range(width // step_n):
            start = half * width + n * step_n
            cols = pl.ds(pl.multiple_of(start, step_n), step_n)
            code = codes[rows, cols]
            lower = jnp.bitwise_and(code, 127)
            exponent = lax.shift_right_logical(lower, 3)
            mantissa = jnp.bitwise_and(lower, 7)
            normal = exponent > 0
            significand = jnp.where(normal, mantissa + 8, mantissa)
            significand = jnp.where(code >= 128, -significand, significand)
            shift = jnp.where(normal, exponent - 1, 0)
            whole = lax.shift_left(significand, shift).astype(F32)
            acts[block, half, h, unit_rows, n * step_n : (n + 1) * step_n] = (
                whole * factors[rows, cols]
            ).astype(BF)
        return carry

    def remote(src, dst, send, recv, tok, ten):
        pltpu.make_async_remote_copy(
            src_ref=src,
            dst_ref=dst,
            send_sem=send,
            recv_sem=recv,
            device_id=(tok, ten),
            device_id_type=MESH,
        ).start()

    def wait(ref, sem):
        pltpu.make_async_copy(ref, ref, sem).wait()

    def several(n, first=0, last=width):
        return acts.at[0, 0, 0:n, 0:UNIT, first:last]

    def move(s, source, first, last, sem, ten, tok=t):
        part = item(s, source)
        if last - first < width:
            part = part.at[:, first:last]
        remote(part, part, send_sem.at[s], sem.at[s], tok, ten)

    def share(s, source):
        move(s, source, 0, width, near_sem, sibling)

    def send_own(s):
        move(s, h, 0, width, x_sem, x_peer, t_other)
        move(s, h, 0, width, z_sem, up)
        move(s, h, 0, width, z_sem, down)
        share(s, h)

    def forward(s):
        wait(several(2), z_sem.at[s])
        move(s, down, 0, middle, z2_sem, up)
        move(s, up, middle, width, z2_sem, down)
        move(s, up, part_a, width, b_sem, x_peer, t_other)
        move(s, down, part_a, width, b_sem, x_peer, t_other)
        wait(several(1), x_sem.at[s])
        move(s, x_peer, 0, part_a, a_sem, up)
        move(s, x_peer, 0, part_a, a_sem, down)
        for source in (up, down, x_peer):
            share(s, source)

    def forward_second(s):
        wait(several(1), z2_sem.at[s])
        move(s, across, part_a, width, b2_sem, x_peer, t_other)
        wait(several(2, 0, part_a), a_sem.at[s])
        move(s, far_down, 0, middle_a, a2_sem, up)
        move(s, far_up, middle_a, part_a, a2_sem, down)
        wait(several(2, part_a, width), b_sem.at[s])
        for source in (across, far_up, far_down):
            share(s, source)

    def forward_third(s):
        wait(several(1, 0, part_a), a2_sem.at[s])
        wait(several(1, part_a, width), b2_sem.at[s])
        share(s, far_across)

    decode(0, 0)
    pl.semaphore_wait(barrier, 11)
    for s in range(AHEAD):
        if s > 0:
            decode(s, 0)
        send_own(s)

    stack[...] = jnp.zeros_like(stack)
    for i, copy in enumerate(fast_copies):
        copy.wait()
        stack[i * head : (i + 1) * head, 0:head] = first_weights[i, 0]
    fast[0] = stack[...].astype(BF)
    for part in range(2):
        own_rows = pl.ds(pl.multiple_of((part * shards + t) * SUB, SUB), SUB)
        master[part] = stack[own_rows, 0:head]
    stack[...] = jnp.zeros_like(stack)
    gains[...] = jnp.broadcast_to(gain_ref[...][None, :], (128, head)).T

    def turn(version):
        gate_lift[version, 0:head] = flip(fast[version, 0:head, 0:head])
        gate_lift[version, head : 2 * head] = flip(fast[version, head : 2 * head, 0:head])

    turn(0)
    w_copy.wait()
    rate_copy.wait()

    def project_keys(c):
        block, half, rows = place(c)

        def one(k, carry):
            cols = pl.ds(pl.multiple_of(k * chunk, chunk), chunk)
            deep = pl.ds(pl.multiple_of(half * width + k * chunk, chunk), chunk)
            x = acts[block, half, :, rows, cols].reshape(tokens, chunk)
            kv_acc[...] += dot_nt(w[head : w.shape[0], deep], x)
            return carry

        @pl.when(half == 0)
        def _():
            kv_acc[...] = jnp.zeros_like(kv_acc)

        lax.fori_loop(0, width // chunk, one, 0)

    def project_queries(c):
        block, half, rows = place(c)

        def one(k, carry):
            cols = pl.ds(pl.multiple_of(k * chunk, chunk), chunk)
            deep = pl.ds(pl.multiple_of(half * width + k * chunk, chunk), chunk)
            x = acts[block, half, :, rows, cols].reshape(tokens, chunk)
            q_acc[...] += dot_nt(w[0:head, deep], x)
            return carry

        @pl.when(half == 0)
        def _():
            q_acc[...] = jnp.zeros_like(q_acc)

        lax.fori_loop(0, width // chunk, one, 0)

    def finish_queries(u):
        block = u // per
        rows = pl.ds(pl.multiple_of((u % per) * UNIT, UNIT), UNIT)
        q = q_acc[...]
        q = q * lax.rsqrt(jnp.sum(q * q, axis=0, keepdims=True) * (1.0 / head) + epsilon)
        made[block, :, rows, 0:head] = q.T.astype(BF).reshape(sources, UNIT, head)
        for k in range(4):
            theirs = pl.ds(k * 4 + (1 - hi) * 2, 2)
            remote(
                made.at[block, theirs, rows],
                queries.at[block, theirs, rows],
                q_send_sem.at[u],
                q_sem.at[u],
                t_other,
                h,
            )
            mine = pl.ds(k * 4 + hi * 2, 2)
            queries[block, mine, rows] = made[block, mine, rows]

    def wait_queries(u):
        sample = queries.at[0, 0:8, 0:UNIT]
        wait(sample, q_sem.at[u])
        wait(sample, q_send_sem.at[u])

    def finish_keys(u):
        k = kv_acc[0:head]
        k = k * lax.rsqrt(jnp.sum(k * k, axis=0, keepdims=True) * (1.0 / head) + epsilon)
        keys[u] = k.astype(BF)
        values[u] = kv_acc[head : 2 * head].astype(BF)
        for i in range(3):
            logit = kv_acc[pl.ds(2 * head + 3 * h + i, 1), :] + bias_ref[0, i]
            soft = jnp.maximum(logit, 0.0) + jnp.log1p(jnp.exp(-jnp.abs(logit)))
            rates[u, i : i + 1] = soft * factor

    def key_step(u, carry):
        version = u // per
        kn = keys[u]
        v = values[u]
        pre = dot(gate_lift[version], kn)
        gate_pre = pre[0:head]
        lift_pre = pre[head : 2 * head]
        hidden_grad = dot(fast[version, 2 * head : 3 * head, 0:head], v)
        sig = jax.nn.sigmoid(gate_pre)
        activated = gate_pre * sig
        hidden = activated * lift_pre
        gate_grad = hidden_grad * lift_pre * (sig * (1.0 + gate_pre * (1.0 - sig)))
        lift_grad = hidden_grad * activated
        gate_grad = (gate_grad * rates[u, 0:1]).astype(BF)
        lift_grad = (lift_grad * rates[u, 1:2]).astype(BF)
        hidden = (hidden * rates[u, 2:3]).astype(BF)
        stack[0:head, 0:head] += dot_nt(kn, gate_grad)
        stack[head : 2 * head, 0:head] += dot_nt(kn, lift_grad)
        stack[2 * head : 3 * head, 0:head] += dot_nt(hidden, v)
        return carry

    def pack(x):
        third = jnp.concatenate(
            [x[0 : SUB // 2, 256 : 256 + PAD], x[SUB // 2 : SUB, 256 : 256 + PAD]], axis=1
        )
        return jnp.concatenate([x[:, 0:128], x[:, 128:256], third], axis=0).astype(BF)

    def unpack(p):
        p = p.astype(F32)
        third = p[2 * SUB : 2 * SUB + SUB // 2]
        third = jnp.concatenate([third[:, 0:PAD], third[:, PAD : 2 * PAD]], axis=0)
        return jnp.concatenate([p[0:SUB], p[SUB : 2 * SUB], third], axis=1)

    def reduce_send(block):
        for part in range(2):

            def pack_one(j, carry, part=part):
                rows = pl.ds(pl.multiple_of((part * shards + j) * SUB, SUB), SUB)
                rs_send[part, j] = pack(stack[rows, :])
                return carry

            lax.fori_loop(0, shards, pack_one, 0)
            for peer in t_peers:
                remote(
                    rs_send.at[part, peer],
                    rs_recv.at[block, part, t],
                    rs_send_sem.at[block, part],
                    rs_sem.at[block, part],
                    peer,
                    h,
                )
            rs_recv[block, part, t] = rs_send[part, t]
        stack[...] = jnp.zeros_like(stack)

    def reduce_finish(block, part):
        wait(rs_recv.at[block, part, 0:7], rs_sem.at[block, part])
        wait(rs_send.at[part, 0:7], rs_send_sem.at[block, part])
        summed = rs_recv[block, part, 0].astype(F32)
        for j in range(1, shards):
            summed = summed + rs_recv[block, part, j].astype(F32)
        old = master[part]
        summed = old + unpack(summed)
        old_scale = jnp.sqrt(
            jnp.sum(old * old, axis=1, keepdims=True) * (1.0 / head) + epsilon
        )
        new_scale = lax.rsqrt(
            jnp.sum(summed * summed, axis=1, keepdims=True) * (1.0 / head) + epsilon
        )
        new = summed * old_scale * new_scale
        master[part] = new
        gathered[block, part, t] = pack(new)
        mine = gathered.at[block, part, t]
        for peer in t_peers:
            remote(
                mine, mine, ag_send_sem.at[block, part], ag_sem.at[block, part], peer, h
            )

    def gather_finish(block):
        for part in range(2):
            wait(gathered.at[block, part, 0:7], ag_sem.at[block, part])

            def unpack_one(j, carry, part=part):
                rows = pl.ds(pl.multiple_of((part * shards + j) * SUB, SUB), SUB)
                fast[block + 1, rows, 0:head] = unpack(gathered[block, part, j]).astype(BF)
                return carry

            lax.fori_loop(0, shards, unpack_one, 0)

    def gather_drain(block):
        for part in range(2):
            wait(gathered.at[block, part, 0:7], ag_send_sem.at[block, part])

    def query_pass(block):
        version = block + 1
        down = flip(fast[version, 2 * head : 3 * head, 0:head])
        gain = jnp.concatenate([gains[...], gains[...]], axis=1)
        for j in range(per):
            wait_queries(block * per + j)
        flat = queries[block].reshape(block_tokens, KEYS)
        for n in range(block_tokens // 256):
            span = slice(n * 256, (n + 1) * 256)
            q = flat[span, 0:head]
            gate_pre = dot(q, fast[version, 0:head, 0:head])
            lift_pre = dot(q, fast[version, head : 2 * head, 0:head])
            hidden = (gate_pre * jax.nn.sigmoid(gate_pre) * lift_pre).astype(BF)
            out = dot_nt(down, hidden)
            out = out * lax.rsqrt(
                jnp.sum(out * out, axis=0, keepdims=True) * (1.0 / head) + epsilon
            )
            out_ref[block, :, span] = (out * gain).astype(BF)

    per_block = rounds // 2

    def step(s, carry):
        @pl.when(s + AHEAD < rounds)
        def _():
            decode(s + AHEAD, 0)
            send_own(s + AHEAD)

        @pl.when(s < rounds)
        def _():
            forward(s)

        c = s - LAG
        half = c % HALVES
        u = c // HALVES

        @pl.when(c >= 0)
        def _():
            wait(several(8), near_sem.at[c])
            project_keys(c)

        @pl.when((s >= 1) & (s < rounds + 1))
        def _():
            forward_second(s - 1)

        @pl.when((c >= 0) & (c < rounds - HALVES))
        def _():
            project_queries(c)

            @pl.when(half == HALVES - 1)
            def _():
                finish_queries(u)

        @pl.when((c >= 0) & (half == HALVES - 1))
        def _():
            finish_keys(u)

        @pl.when((s >= 2) & (s < rounds + 2))
        def _():
            forward_third(s - 2)

        @pl.when(c == per_block + 1)
        def _():
            reduce_finish(0, 0)

        @pl.when(c == per_block + 2)
        def _():
            reduce_finish(0, 1)

        @pl.when(c == per_block + 4)
        def _():
            gather_finish(0)
            turn(1)

        begin = per_block + 4
        usual = (c >= 0) & (half == HALVES - 1) & ((c < per_block) | (c > begin))
        first = jnp.where(c == begin, per, u)
        last = jnp.where(c == begin, (begin + 1) // HALVES, jnp.where(usual, u + 1, u))
        lax.fori_loop(first, last, key_step, 0)

        @pl.when(c == per_block - 1)
        def _():
            reduce_send(0)

        return carry

    lax.fori_loop(0, rounds + LAG, step, 0)
    reduce_send(1)
    for half in range(HALVES):
        project_queries(rounds - HALVES + half)
    finish_queries(units - 1)
    gather_drain(0)
    reduce_finish(1, 0)
    reduce_finish(1, 1)
    query_pass(0)

    def drain(s, carry):
        wait(several(15), send_sem.at[s])
        return carry

    lax.fori_loop(0, rounds, drain, 0)
    gather_finish(1)
    query_pass(1)
    gather_drain(1)


def local(codes, scales, w_qkv, w_rate, rate_bias, fast_gate, fast_lift, fast_down, out_gain):
    blocks, rows, depth = codes.shape
    head = fast_gate.shape[1]
    sources = lax.axis_size("tensor")
    shards = lax.axis_size("tokens")
    units = blocks * rows // UNIT
    rounds = units * HALVES
    tokens = sources * UNIT
    width = depth // HALVES
    factor = rate_base / math.sqrt(rows * sources * shards)
    stacked = 3 * head + PAD
    columns = w_qkv.shape[1] + w_rate.shape[1]
    vmem = pl.BlockSpec(memory_space=pltpu.VMEM)
    smem = pl.BlockSpec(memory_space=pltpu.SMEM)
    anyspace = pl.BlockSpec(memory_space=pl.ANY)
    dma = pltpu.SemaphoreType.DMA
    out = pl.pallas_call(
        functools.partial(kernel, factor),
        out_shape=jax.ShapeDtypeStruct((blocks, head, sources * rows), BF),
        in_specs=[anyspace, vmem, anyspace, anyspace, smem] + [anyspace] * 3 + [vmem],
        out_specs=vmem,
        scratch_shapes=[
            pltpu.VMEM((blocks, HALVES, sources, rows, width), BF),
            pltpu.VMEM((columns, depth), BF),
            pltpu.VMEM((blocks * rows, depth), jnp.int32),
            pltpu.VMEM((scales.shape[2], depth), BF),
            pltpu.VMEM((blocks * rows, depth), F32),
            pltpu.VMEM((columns - head, tokens), F32),
            pltpu.VMEM((head, tokens), F32),
            pltpu.VMEM((stacked, KEYS), F32),
            pltpu.VMEM((2, SUB, head), F32),
            pltpu.VMEM((2, shards, SUB * 5 // 2, 128), BF),
            pltpu.VMEM((2, 2, shards, SUB * 5 // 2, 128), BF),
            pltpu.VMEM((2, 2, shards, SUB * 5 // 2, 128), BF),
            pltpu.VMEM((3, 1, head, head), F32),
            pltpu.VMEM((3, stacked, KEYS), BF),
            pltpu.VMEM((2, 2 * head, head), BF),
            pltpu.VMEM((head, 128), F32),
            pltpu.VMEM((blocks, sources, rows, KEYS), BF),
            pltpu.VMEM((blocks, sources, rows, KEYS), BF),
            pltpu.VMEM((units, head, tokens), BF),
            pltpu.VMEM((units, head, tokens), BF),
            pltpu.VMEM((units, 8, tokens), F32),
            dma((6,)),
            dma((rounds,)),
            dma((rounds,)),
            dma((rounds,)),
            dma((rounds,)),
            dma((rounds,)),
            dma((rounds,)),
            dma((rounds,)),
            dma((rounds,)),
            dma((rounds,)),
            dma((units,)),
            dma((units,)),
            dma((2, 2)),
            dma((2, 2)),
            dma((2, 2)),
            dma((2, 2)),
        ],
        compiler_params=pltpu.CompilerParams(
            collective_id=0, has_side_effects=True, vmem_limit_bytes=58 << 20
        ),
        name="fast_weights",
    )(
        codes.reshape(blocks * rows, depth),
        scales.reshape(blocks * rows, scales.shape[2]),
        w_qkv.T,
        w_rate.T,
        rate_bias.reshape(1, 3),
        fast_gate,
        fast_lift,
        fast_down,
        out_gain,
    )
    return jnp.transpose(out, (0, 2, 1))


def solution(mesh):
    return jax.shard_map(
        local,
        mesh=mesh,
        in_specs=(
            P(None, ("tokens", "tensor"), None),
            P(None, ("tokens", "tensor"), None),
            P(None, "tensor"),
            P(),
            P("tensor"),
            P("tensor", None, None),
            P("tensor", None, None),
            P("tensor", None, None),
            P("tensor"),
        ),
        out_specs=P(None, "tokens", "tensor"),
        check_vma=False,
    )
```

```python
import functools
import math

import jax
import jax.numpy as jnp
from jax import lax
from jax.experimental import pallas as pl
from jax.experimental.pallas import tpu as pltpu
from jax.sharding import PartitionSpec as P

epsilon = 1e-06
rate_base = 0.15

MESH = pl.DeviceIdType.MESH
BF = jnp.bfloat16
F32 = jnp.float32

UNIT = 16
HALVES = 2
AHEAD = 1
LAG = 3
KEYS = 384
SUB = 64
PAD = 64


def dot(a, b):
    return jnp.dot(a, b, preferred_element_type=F32)


def dot_nt(a, b):
    return lax.dot_general(a, b, (((1,), (1,)), ((), ())), preferred_element_type=F32)


def flip(a):
    return a.astype(F32).T.astype(BF)


def kernel(
    factor,
    codes_hbm,
    scales_ref,
    wqkv_hbm,
    wrate_hbm,
    bias_ref,
    gate_ref,
    lift_ref,
    down_ref,
    gain_ref,
    out_ref,
    acts,
    w,
    codes,
    spread,
    factors,
    kv_acc,
    q_acc,
    stack,
    master,
    rs_send,
    rs_recv,
    gathered,
    first_weights,
    fast,
    gate_lift,
    gains,
    made,
    queries,
    keys,
    values,
    rates,
    local_sem,
    send_sem,
    z_sem,
    z2_sem,
    x_sem,
    a_sem,
    a2_sem,
    b_sem,
    b2_sem,
    near_sem,
    q_send_sem,
    q_sem,
    rs_send_sem,
    rs_sem,
    ag_send_sem,
    ag_sem,
):
    blocks, _, sources, rows_dev, width = acts.shape
    per = rows_dev // UNIT
    units = blocks * per
    rounds = units * HALVES
    part_a = width * 5 // 9 // 128 * 128
    middle = width // 256 * 128
    middle_a = part_a // 256 * 128
    depth = w.shape[1]
    head = gate_ref.shape[1]
    tokens = sources * UNIT
    block_tokens = sources * rows_dev
    chunk = 1280
    t = lax.axis_index("tokens")
    h = lax.axis_index("tensor")
    shards = 8
    z, hi, core = h // 4, (h // 2) % 2, h % 2

    def at(dz, other):
        side = 1 - hi if other else hi
        return lax.rem(z + dz, 4) * 4 + side * 2 + core

    up, down, across = at(1, False), at(3, False), at(2, False)
    x_peer, t_other = at(0, True), lax.rem(t + 4, shards)
    far_up, far_down, far_across = at(1, True), at(3, True), at(2, True)
    sibling = h + 1 - 2 * core
    t_peers = [lax.rem(t + k, shards) for k in range(1, shards)]

    barrier = pltpu.get_barrier_semaphore()
    for peer in (up, down, sibling):
        pl.semaphore_signal(barrier, inc=1, device_id=(t, peer), device_id_type=MESH)
    pl.semaphore_signal(barrier, inc=1, device_id=(t_other, x_peer), device_id_type=MESH)
    for peer in t_peers:
        pl.semaphore_signal(barrier, inc=1, device_id=(peer, h), device_id_type=MESH)

    codes_copy = pltpu.make_async_copy(codes_hbm, codes, local_sem.at[0])
    w_copy = pltpu.make_async_copy(wqkv_hbm, w.at[0 : 3 * head], local_sem.at[1])
    rate_copy = pltpu.make_async_copy(
        wrate_hbm, w.at[3 * head : w.shape[0]], local_sem.at[2]
    )
    codes_copy.start()
    fast_copies = [
        pltpu.make_async_copy(ref, first_weights.at[i], local_sem.at[3 + i])
        for i, ref in enumerate((gate_ref, lift_ref, down_ref))
    ]
    for copy in fast_copies:
        copy.start()
    w_copy.start()
    rate_copy.start()

    groups = scales_ref.shape[1]
    group = lax.broadcasted_iota(jnp.int32, (groups, depth), 0)
    column = lax.broadcasted_iota(jnp.int32, (groups, depth), 1)
    spread[...] = jnp.where(
        lax.shift_right_logical(column, 5) == group, 1.0, 0.0
    ).astype(BF)
    powers = lax.shift_left(jnp.ones_like(scales_ref[...]), scales_ref[...] - 119)
    powers = powers.astype(F32).astype(BF)
    step_n = 512

    def spread_step(n, carry):
        cols = pl.ds(pl.multiple_of(n * step_n, step_n), step_n)
        factors[:, cols] = dot(powers, spread[:, cols]) * (1.0 / 131072.0)
        return carry

    lax.fori_loop(0, depth // step_n, spread_step, 0)
    codes_copy.wait()

    def place(s):
        u = s // HALVES
        return u // per, s % HALVES, pl.ds(pl.multiple_of((u % per) * UNIT, UNIT), UNIT)

    def item(s, source):
        block, half, rows = place(s)
        return acts.at[block, half, source, rows]

    def decode(s, carry):
        block, half, unit_rows = place(s)
        rows = pl.ds(pl.multiple_of((s // HALVES) * UNIT, UNIT), UNIT)
        for n in range(width // step_n):
            start = half * width + n * step_n
            cols = pl.ds(pl.multiple_of(start, step_n), step_n)
            code = codes[rows, cols]
            lower = jnp.bitwise_and(code, 127)
            exponent = lax.shift_right_logical(lower, 3)
            mantissa = jnp.bitwise_and(lower, 7)
            normal = exponent > 0
            significand = jnp.where(normal, mantissa + 8, mantissa)
            significand = jnp.where(code >= 128, -significand, significand)
            shift = jnp.where(normal, exponent - 1, 0)
            whole = lax.shift_left(significand, shift).astype(F32)
            acts[block, half, h, unit_rows, n * step_n : (n + 1) * step_n] = (
                whole * factors[rows, cols]
            ).astype(BF)
        return carry

    def remote(src, dst, send, recv, tok, ten):
        pltpu.make_async_remote_copy(
            src_ref=src,
            dst_ref=dst,
            send_sem=send,
            recv_sem=recv,
            device_id=(tok, ten),
            device_id_type=MESH,
        ).start()

    def wait(ref, sem):
        pltpu.make_async_copy(ref, ref, sem).wait()

    def several(n, first=0, last=width):
        return acts.at[0, 0, 0:n, 0:UNIT, first:last]

    def move(s, source, first, last, sem, ten, tok=t):
        part = item(s, source)
        if last - first < width:
            part = part.at[:, first:last]
        remote(part, part, send_sem.at[s], sem.at[s], tok, ten)

    def share(s, source):
        move(s, source, 0, width, near_sem, sibling)

    def send_own(s):
        move(s, h, 0, width, x_sem, x_peer, t_other)
        move(s, h, 0, width, z_sem, up)
        move(s, h, 0, width, z_sem, down)
        share(s, h)

    def forward(s):
        wait(several(2), z_sem.at[s])
        move(s, down, 0, middle, z2_sem, up)
        move(s, up, middle, width, z2_sem, down)
        move(s, up, part_a, width, b_sem, x_peer, t_other)
        move(s, down, part_a, width, b_sem, x_peer, t_other)
        wait(several(1), x_sem.at[s])
        move(s, x_peer, 0, part_a, a_sem, up)
        move(s, x_peer, 0, part_a, a_sem, down)
        for source in (up, down, x_peer):
            share(s, source)

    def forward_second(s):
        wait(several(1), z2_sem.at[s])
        move(s, across, part_a, width, b2_sem, x_peer, t_other)
        wait(several(2, 0, part_a), a_sem.at[s])
        move(s, far_down, 0, middle_a, a2_sem, up)
        move(s, far_up, middle_a, part_a, a2_sem, down)
        wait(several(2, part_a, width), b_sem.at[s])
        for source in (across, far_up, far_down):
            share(s, source)

    def forward_third(s):
        wait(several(1, 0, part_a), a2_sem.at[s])
        wait(several(1, part_a, width), b2_sem.at[s])
        share(s, far_across)

    decode(0, 0)
    pl.semaphore_wait(barrier, 11)
    for s in range(AHEAD):
        if s > 0:
            decode(s, 0)
        send_own(s)

    stack[...] = jnp.zeros_like(stack)
    for i, copy in enumerate(fast_copies):
        copy.wait()
        stack[i * head : (i + 1) * head, 0:head] = first_weights[i, 0]
    fast[0] = stack[...].astype(BF)
    for part in range(2):
        own_rows = pl.ds(pl.multiple_of((part * shards + t) * SUB, SUB), SUB)
        master[part] = stack[own_rows, 0:head]
    stack[...] = jnp.zeros_like(stack)
    gains[...] = jnp.broadcast_to(gain_ref[...][None, :], (128, head)).T

    def turn(version):
        gate_lift[version, 0:head] = flip(fast[version, 0:head, 0:head])
        gate_lift[version, head : 2 * head] = flip(fast[version, head : 2 * head, 0:head])

    turn(0)
    w_copy.wait()
    rate_copy.wait()

    def project_keys(c):
        block, half, rows = place(c)

        def one(k, carry):
            cols = pl.ds(pl.multiple_of(k * chunk, chunk), chunk)
            deep = pl.ds(pl.multiple_of(half * width + k * chunk, chunk), chunk)
            x = acts[block, half, :, rows, cols].reshape(tokens, chunk)
            kv_acc[...] += dot_nt(w[head : w.shape[0], deep], x)
            return carry

        @pl.when(half == 0)
        def _():
            kv_acc[...] = jnp.zeros_like(kv_acc)

        lax.fori_loop(0, width // chunk, one, 0)

    def project_queries(c):
        block, half, rows = place(c)

        def one(k, carry):
            cols = pl.ds(pl.multiple_of(k * chunk, chunk), chunk)
            deep = pl.ds(pl.multiple_of(half * width + k * chunk, chunk), chunk)
            x = acts[block, half, :, rows, cols].reshape(tokens, chunk)
            q_acc[...] += dot_nt(w[0:head, deep], x)
            return carry

        @pl.when(half == 0)
        def _():
            q_acc[...] = jnp.zeros_like(q_acc)

        lax.fori_loop(0, width // chunk, one, 0)

    def finish_queries(u):
        block = u // per
        rows = pl.ds(pl.multiple_of((u % per) * UNIT, UNIT), UNIT)
        q = q_acc[...]
        q = q * lax.rsqrt(jnp.sum(q * q, axis=0, keepdims=True) * (1.0 / head) + epsilon)
        made[block, :, rows, 0:head] = q.T.astype(BF).reshape(sources, UNIT, head)
        for k in range(4):
            theirs = pl.ds(k * 4 + (1 - hi) * 2, 2)
            remote(
                made.at[block, theirs, rows],
                queries.at[block, theirs, rows],
                q_send_sem.at[u],
                q_sem.at[u],
                t_other,
                h,
            )
            mine = pl.ds(k * 4 + hi * 2, 2)
            queries[block, mine, rows] = made[block, mine, rows]

    def wait_queries(u):
        sample = queries.at[0, 0:8, 0:UNIT]
        wait(sample, q_sem.at[u])
        wait(sample, q_send_sem.at[u])

    def finish_keys(u):
        k = kv_acc[0:head]
        k = k * lax.rsqrt(jnp.sum(k * k, axis=0, keepdims=True) * (1.0 / head) + epsilon)
        keys[u] = k.astype(BF)
        values[u] = kv_acc[head : 2 * head].astype(BF)
        for i in range(3):
            logit = kv_acc[pl.ds(2 * head + 3 * h + i, 1), :] + bias_ref[0, i]
            soft = jnp.maximum(logit, 0.0) + jnp.log1p(jnp.exp(-jnp.abs(logit)))
            rates[u, i : i + 1] = soft * factor

    def key_step(u, carry):
        version = u // per
        kn = keys[u]
        v = values[u]
        pre = dot(gate_lift[version], kn)
        gate_pre = pre[0:head]
        lift_pre = pre[head : 2 * head]
        hidden_grad = dot(fast[version, 2 * head : 3 * head, 0:head], v)
        sig = jax.nn.sigmoid(gate_pre)
        activated = gate_pre * sig
        hidden = activated * lift_pre
        gate_grad = hidden_grad * lift_pre * (sig * (1.0 + gate_pre * (1.0 - sig)))
        lift_grad = hidden_grad * activated
        gate_grad = (gate_grad * rates[u, 0:1]).astype(BF)
        lift_grad = (lift_grad * rates[u, 1:2]).astype(BF)
        hidden = (hidden * rates[u, 2:3]).astype(BF)
        stack[0:head, 0:head] += dot_nt(kn, gate_grad)
        stack[head : 2 * head, 0:head] += dot_nt(kn, lift_grad)
        stack[2 * head : 3 * head, 0:head] += dot_nt(hidden, v)
        return carry

    def pack(x):
        third = jnp.concatenate(
            [x[0 : SUB // 2, 256 : 256 + PAD], x[SUB // 2 : SUB, 256 : 256 + PAD]], axis=1
        )
        return jnp.concatenate([x[:, 0:128], x[:, 128:256], third], axis=0).astype(BF)

    def unpack(p):
        p = p.astype(F32)
        third = p[2 * SUB : 2 * SUB + SUB // 2]
        third = jnp.concatenate([third[:, 0:PAD], third[:, PAD : 2 * PAD]], axis=0)
        return jnp.concatenate([p[0:SUB], p[SUB : 2 * SUB], third], axis=1)

    def reduce_send(block):
        for part in range(2):

            def pack_one(j, carry, part=part):
                rows = pl.ds(pl.multiple_of((part * shards + j) * SUB, SUB), SUB)
                rs_send[part, j] = pack(stack[rows, :])
                return carry

            lax.fori_loop(0, shards, pack_one, 0)
            for peer in t_peers:
                remote(
                    rs_send.at[part, peer],
                    rs_recv.at[block, part, t],
                    rs_send_sem.at[block, part],
                    rs_sem.at[block, part],
                    peer,
                    h,
                )
            rs_recv[block, part, t] = rs_send[part, t]
        stack[...] = jnp.zeros_like(stack)

    def reduce_finish(block, part):
        wait(rs_recv.at[block, part, 0:7], rs_sem.at[block, part])
        wait(rs_send.at[part, 0:7], rs_send_sem.at[block, part])
        summed = rs_recv[block, part, 0].astype(F32)
        for j in range(1, shards):
            summed = summed + rs_recv[block, part, j].astype(F32)
        old = master[part]
        summed = old + unpack(summed)
        old_scale = jnp.sqrt(
            jnp.sum(old * old, axis=1, keepdims=True) * (1.0 / head) + epsilon
        )
        new_scale = lax.rsqrt(
            jnp.sum(summed * summed, axis=1, keepdims=True) * (1.0 / head) + epsilon
        )
        new = summed * old_scale * new_scale
        master[part] = new
        gathered[block, part, t] = pack(new)
        mine = gathered.at[block, part, t]
        for peer in t_peers:
            remote(
                mine, mine, ag_send_sem.at[block, part], ag_sem.at[block, part], peer, h
            )

    def gather_finish(block):
        for part in range(2):
            wait(gathered.at[block, part, 0:7], ag_sem.at[block, part])

            def unpack_one(j, carry, part=part):
                rows = pl.ds(pl.multiple_of((part * shards + j) * SUB, SUB), SUB)
                fast[block + 1, rows, 0:head] = unpack(gathered[block, part, j]).astype(BF)
                return carry

            lax.fori_loop(0, shards, unpack_one, 0)

    def gather_drain(block):
        for part in range(2):
            wait(gathered.at[block, part, 0:7], ag_send_sem.at[block, part])

    def query_pass(block):
        version = block + 1
        down = flip(fast[version, 2 * head : 3 * head, 0:head])
        gain = jnp.concatenate([gains[...], gains[...]], axis=1)
        for j in range(per):
            wait_queries(block * per + j)
        flat = queries[block].reshape(block_tokens, KEYS)
        for n in range(block_tokens // 256):
            span = slice(n * 256, (n + 1) * 256)
            q = flat[span, 0:head]
            gate_pre = dot(q, fast[version, 0:head, 0:head])
            lift_pre = dot(q, fast[version, head : 2 * head, 0:head])
            hidden = (gate_pre * jax.nn.sigmoid(gate_pre) * lift_pre).astype(BF)
            out = dot_nt(down, hidden)
            out = out * lax.rsqrt(
                jnp.sum(out * out, axis=0, keepdims=True) * (1.0 / head) + epsilon
            )
            out_ref[block, :, span] = (out * gain).astype(BF)

    per_block = rounds // 2

    def step(s, carry):
        @pl.when(s + AHEAD < rounds)
        def _():
            decode(s + AHEAD, 0)
            send_own(s + AHEAD)

        c = s - LAG
        half = c % HALVES
        u = c // HALVES

        @pl.when(c >= 0)
        def _():
            wait(several(8), near_sem.at[c])
            project_keys(c)

        @pl.when(s < rounds)
        def _():
            forward(s)

        @pl.when((c >= 0) & (c < rounds - HALVES))
        def _():
            project_queries(c)

            @pl.when(half == HALVES - 1)
            def _():
                finish_queries(u)

        @pl.when((s >= 1) & (s < rounds + 1))
        def _():
            forward_second(s - 1)

        @pl.when((c >= 0) & (half == HALVES - 1))
        def _():
            finish_keys(u)

        @pl.when((s >= 2) & (s < rounds + 2))
        def _():
            forward_third(s - 2)

        @pl.when(c == per_block + 1)
        def _():
            reduce_finish(0, 0)

        @pl.when(c == per_block + 2)
        def _():
            reduce_finish(0, 1)

        @pl.when(c == per_block + 4)
        def _():
            gather_finish(0)
            turn(1)

        begin = per_block + 4
        usual = (c >= 0) & (half == HALVES - 1) & ((c < per_block) | (c > begin))
        first = jnp.where(c == begin, per, u)
        last = jnp.where(c == begin, (begin + 1) // HALVES, jnp.where(usual, u + 1, u))
        lax.fori_loop(first, last, key_step, 0)

        @pl.when(c == per_block - 1)
        def _():
            reduce_send(0)

        return carry

    lax.fori_loop(0, rounds + LAG, step, 0)
    reduce_send(1)
    for half in range(HALVES):
        project_queries(rounds - HALVES + half)
    finish_queries(units - 1)
    gather_drain(0)
    reduce_finish(1, 0)
    reduce_finish(1, 1)
    query_pass(0)

    def drain(s, carry):
        wait(several(15), send_sem.at[s])
        return carry

    lax.fori_loop(0, rounds, drain, 0)
    gather_finish(1)
    query_pass(1)
    gather_drain(1)


def local(codes, scales, w_qkv, w_rate, rate_bias, fast_gate, fast_lift, fast_down, out_gain):
    blocks, rows, depth = codes.shape
    head = fast_gate.shape[1]
    sources = lax.axis_size("tensor")
    shards = lax.axis_size("tokens")
    units = blocks * rows // UNIT
    rounds = units * HALVES
    tokens = sources * UNIT
    width = depth // HALVES
    factor = rate_base / math.sqrt(rows * sources * shards)
    stacked = 3 * head + PAD
    columns = w_qkv.shape[1] + w_rate.shape[1]
    vmem = pl.BlockSpec(memory_space=pltpu.VMEM)
    smem = pl.BlockSpec(memory_space=pltpu.SMEM)
    anyspace = pl.BlockSpec(memory_space=pl.ANY)
    dma = pltpu.SemaphoreType.DMA
    out = pl.pallas_call(
        functools.partial(kernel, factor),
        out_shape=jax.ShapeDtypeStruct((blocks, head, sources * rows), BF),
        in_specs=[anyspace, vmem, anyspace, anyspace, smem] + [anyspace] * 3 + [vmem],
        out_specs=vmem,
        scratch_shapes=[
            pltpu.VMEM((blocks, HALVES, sources, rows, width), BF),
            pltpu.VMEM((columns, depth), BF),
            pltpu.VMEM((blocks * rows, depth), jnp.int32),
            pltpu.VMEM((scales.shape[2], depth), BF),
            pltpu.VMEM((blocks * rows, depth), F32),
            pltpu.VMEM((columns - head, tokens), F32),
            pltpu.VMEM((head, tokens), F32),
            pltpu.VMEM((stacked, KEYS), F32),
            pltpu.VMEM((2, SUB, head), F32),
            pltpu.VMEM((2, shards, SUB * 5 // 2, 128), BF),
            pltpu.VMEM((2, 2, shards, SUB * 5 // 2, 128), BF),
            pltpu.VMEM((2, 2, shards, SUB * 5 // 2, 128), BF),
            pltpu.VMEM((3, 1, head, head), F32),
            pltpu.VMEM((3, stacked, KEYS), BF),
            pltpu.VMEM((2, 2 * head, head), BF),
            pltpu.VMEM((head, 128), F32),
            pltpu.VMEM((blocks, sources, rows, KEYS), BF),
            pltpu.VMEM((blocks, sources, rows, KEYS), BF),
            pltpu.VMEM((units, head, tokens), BF),
            pltpu.VMEM((units, head, tokens), BF),
            pltpu.VMEM((units, 8, tokens), F32),
            dma((6,)),
            dma((rounds,)),
            dma((rounds,)),
            dma((rounds,)),
            dma((rounds,)),
            dma((rounds,)),
            dma((rounds,)),
            dma((rounds,)),
            dma((rounds,)),
            dma((rounds,)),
            dma((units,)),
            dma((units,)),
            dma((2, 2)),
            dma((2, 2)),
            dma((2, 2)),
            dma((2, 2)),
        ],
        compiler_params=pltpu.CompilerParams(
            collective_id=0, has_side_effects=True, vmem_limit_bytes=58 << 20
        ),
        name="fast_weights",
    )(
        codes.reshape(blocks * rows, depth),
        scales.reshape(blocks * rows, scales.shape[2]),
        w_qkv.T,
        w_rate.T,
        rate_bias.reshape(1, 3),
        fast_gate,
        fast_lift,
        fast_down,
        out_gain,
    )
    return jnp.transpose(out, (0, 2, 1))


def solution(mesh):
    return jax.shard_map(
        local,
        mesh=mesh,
        in_specs=(
            P(None, ("tokens", "tensor"), None),
            P(None, ("tokens", "tensor"), None),
            P(None, "tensor"),
            P(),
            P("tensor"),
            P("tensor", None, None),
            P("tensor", None, None),
            P("tensor", None, None),
            P("tensor"),
        ),
        out_specs=P(None, "tokens", "tensor"),
        check_vma=False,
    )
```
